512 devices in a mesh: dp: 32 (over x, z_hi, core), tensor: 16 (over z_lo, y).
Axes of the slice: x: 4, y: 4, z: 16 (z_hi: 4, z_lo: 4; z = z_hi * 4 + z_lo), core: 2. Of those that a mesh axis runs over, the one named last changes fastest.
Arguments:
- activations: bfloat16 [640, 26624], P('dp', 'tensor'), may hold values from -6 to 6
- weight_codes: int32 [26624, 8192], P(('tensor', 'dp')), may hold values from 0 to 15
- scale_index: int32 [26624, 64], P(('tensor', 'dp')), may hold values from 0 to 15, as said below
- scale_table: float32 [16], replicated
- bit_widths: int32 [1, 26624, 64], P(None, ('tensor', 'dp')), may hold values from 2 to 4
Outputs:
- base_output: bfloat16 [640, 8192], P('tensor', 'dp')
- scores: float32 [1, 640], P(None, 'tensor')
The draws below stay inside these ranges and needn't reach their ends.
Inputs may be any that keep to these rules, and one draw needn't show every extreme that they name: `scale_index`: an entry of scale_table for each row and each group of 128 columns.
All inputs are finite; a program needn't handle non-finite values.
Results may differ from the reference program's by a relative error of at most 0.0058.
Values may be sent and summed in bfloat16 or wider, within the bound.
No kernel may reach another device: no remote copies, remote signals or barrier semaphores. Data moves between devices by JAX's collectives and lax.ppermute only.
A program may use at most 64 MiB of HBM per device.

```python
import math
import jax
import jax.numpy as jnp
from jax import lax

D = 8192
FF_DEV = 1664
HB = 128
GROUP = 128
NSCALE = 16
NCAND = 1
FFW = 26624
TOKENS = 640
NGRP = 64
N_TENSOR = 16


def draw_scale_index(key, part):
    noise = jax.random.randint(key, (FFW, NGRP), 0, 4)
    level = (NSCALE - 3) * jnp.arange(NGRP, dtype=jnp.int32) // NGRP
    chosen = (noise + level[None, :]).astype(jnp.int32)
    chosen = chosen.at[0, 0].set(0)
    chosen = chosen.at[FFW - 1, NGRP - 1].set(NSCALE - 1)
    return chosen


def draw_scale_table(key, part):
    ladder = jnp.arange(NSCALE, dtype=jnp.float32) / (NSCALE - 1)
    factor = jax.random.uniform(key, (NSCALE,), jnp.float32, 0.8, 1.25)
    return 0.25 * FFW ** (-0.5) * jnp.exp(ladder * jnp.log(3.0)) * factor


def place_ends(entries, rng, smallest, largest):
    longest = entries.shape.index(max(entries.shape))
    spots = []
    for shift in (0, 1):
        where = [jax.random.randint(jax.random.fold_in(rng, axis), (), 0, length) for axis, length in enumerate(entries.shape)]
        where[longest] = (where[longest] + shift) % entries.shape[longest]
        spots.append(tuple(where))
    return entries.at[spots[0]].set(smallest).at[spots[1]].set(largest)


def level_of(key, dims, shards, low, largest):
    def one(axis_at, shards_of):
        draws = jax.random.uniform(jax.random.fold_in(jax.random.fold_in(key, 6), axis_at), (shards_of,), jnp.float32, low / len(shards), largest / len(shards))
        return jnp.repeat(jnp.exp(draws), dims[axis_at] // shards_of).reshape((-1,) + (1,) * (len(dims) - axis_at - 1))

    gain = one(*shards[0])
    for cut in shards[1:]:
        gain = gain * one(*cut)
    return gain


def gaussian(rng, extent, deviation, bound, pieces=(), held_as=jnp.bfloat16):
    result = deviation * jax.random.normal(rng, extent, jnp.float32)
    if pieces:
        result = result * level_of(rng, extent, pieces, -0.22, 0.18)
    return jnp.clip(result, -bound, bound).astype(held_as)


def setup_inputs(seed: int = 0) -> dict:
    seeds = jax.random.split(jax.random.key(seed), 6)
    return {
        "activations": gaussian(seeds[0], (TOKENS, FFW), 1.0, 6.0, ((0, 32), (1, 16))),
        "weight_codes": place_ends(jax.random.randint(seeds[1], (FFW, D), 0, 16), jax.random.fold_in(seeds[1], 1), 0, 15).astype(jnp.int32),
        "scale_index": draw_scale_index(jax.random.fold_in(seeds[5], 71), 0),
        "scale_table": draw_scale_table(jax.random.fold_in(seeds[5], 71), 0),
        "bit_widths": place_ends(jax.random.randint(seeds[4], (NCAND, FFW, NGRP), 2, 5), jax.random.fold_in(seeds[4], 1), 2, 4).astype(jnp.int32),
    }


score_divisor = 512.0

def sylvester(order_size):
    positions = jnp.arange(order_size, dtype=jnp.int32)
    intersection = positions[:, None] & positions[None, :]
    parity = jnp.zeros((order_size, order_size), jnp.int32)
    for shift_bit in range(max(order_size.bit_length() - 1, 0)):
        parity = parity + (intersection >> shift_bit & 1)
    parity = parity % 2
    return (1 - 2 * parity).astype(jnp.float32)

def rotate(activations):
    token_count = activations.shape[0]
    shaped = activations.astype(jnp.float32).reshape(token_count, N_TENSOR, FF_DEV // HB, HB)
    inner = jnp.einsum('tsnb,bc->tsnc', shaped, sylvester(HB), precision=lax.Precision.HIGHEST)
    outer = jnp.einsum('tsnc,js->tjnc', inner, sylvester(N_TENSOR), precision=lax.Precision.HIGHEST)
    scaled = outer * (1.0 / math.sqrt(HB * N_TENSOR))
    return scaled.reshape(token_count, FFW).astype(jnp.bfloat16)

def reference(activations, weight_codes, scale_index, scale_table, bit_widths):
    rotated = rotate(activations)

    def column_block(group_id):
        code_block = lax.dynamic_slice_in_dim(weight_codes, group_id * GROUP, GROUP, 1)
        index_block = lax.dynamic_slice_in_dim(scale_index, group_id, 1, 1)
        scale_block = scale_table[index_block]
        bits_block = lax.dynamic_slice_in_dim(bit_widths, group_id, 1, 2)
        base_weight = ((code_block - 8).astype(jnp.float32) * scale_block).astype(jnp.bfloat16)
        base_out = jnp.dot(rotated, base_weight, preferred_element_type=jnp.float32)
        step_size = jnp.where(bits_block == 2, 4, jnp.where(bits_block == 3, 2, 1)).astype(jnp.int32)
        cand_codes = code_block[None] // step_size * step_size + step_size // 2
        cand_weight = ((cand_codes - 8).astype(jnp.float32) * scale_block[None]).astype(jnp.bfloat16)
        errors = []
        for candidate in range(NCAND):
            cand_out = jnp.dot(rotated, cand_weight[candidate], preferred_element_type=jnp.float32)
            gap = cand_out - base_out
            errors.append(lax.optimization_barrier(jnp.sum(gap * gap, axis=1)) / score_divisor)
        return (base_out, jnp.stack(errors, 0))
    base_blocks, group_scores = lax.map(column_block, jnp.arange(NGRP, dtype=jnp.int32))
    base_output = jnp.transpose(base_blocks, (1, 0, 2)).reshape(TOKENS, D).astype(jnp.bfloat16)
    scores = lax.optimization_barrier(jnp.sum(group_scores, axis=0))
    return (base_output, scores)
```

```python
import math

import jax
import jax.numpy as jnp
from jax import lax
from jax.experimental import pallas as pl
from jax.experimental.pallas import tpu as pltpu
from jax.sharding import Mesh, PartitionSpec as P


HB = 128
GROUP = 128
AXES = ("x", "zh", "c", "zl", "y")
SIZES = (4, 4, 2, 4, 4)
SCORE_DIVISOR = 512.0
F32 = jnp.float32
BF16 = jnp.bfloat16
VMEM = pl.BlockSpec(memory_space=pltpu.VMEM)
SMEM = pl.BlockSpec(memory_space=pltpu.SMEM)


def sylvester(order):
    at = jnp.arange(order, dtype=jnp.int32)
    both = at[:, None] & at[None, :]
    parity = jnp.zeros((order, order), jnp.int32)
    for bit in range(order.bit_length() - 1):
        parity = parity + (both >> bit & 1)
    return (1 - 2 * (parity % 2)).astype(F32)


def call(kernel, out_shape, in_specs, scratch=(), flops=0, moved=0):
    multi = isinstance(out_shape, (list, tuple))
    return pl.pallas_call(
        kernel,
        out_shape=out_shape,
        in_specs=in_specs,
        out_specs=[VMEM] * len(out_shape) if multi else VMEM,
        scratch_shapes=list(scratch),
        cost_estimate=pl.CostEstimate(flops=flops, bytes_accessed=moved, transcendentals=0),
    )


def block_kernel(act, signs, out):
    for n in range(act.shape[1] // HB):
        cols = slice(n * HB, (n + 1) * HB)
        out[:, cols] = jnp.dot(act[:, cols], signs[...], preferred_element_type=F32)


def pack_kernel(codes, index, bits, out, meta, turned, block):
    rows = codes.shape[0]
    parts, _, width = out.shape
    groups = index.shape[1]
    per = groups // parts
    meta[...] = jnp.zeros_like(meta)
    meta[0:rows, 0:groups] = index[...].astype(F32)
    meta[0:rows, groups : 2 * groups] = bits[...].astype(F32)
    turned[...] = meta[...].T
    block[...] = jnp.zeros_like(block)
    for p in range(parts):
        block[0:rows, :] = codes[:, p * width : (p + 1) * width].astype(F32)
        block[rows : rows + per, 0:GROUP] = turned[p * per : (p + 1) * per, :]
        block[rows : rows + per, GROUP : 2 * GROUP] = turned[groups + p * per : groups + (p + 1) * per, :]
        out[p] = block[...].astype(BF16)


def weight_kernel(rows, own, other, table, place, base, diff, meta, base_acc, diff_acc):
    parts, padded, width = own.shape
    per = width // GROUP
    groups = parts * per
    first = place[2] == 0
    turned = []
    for core in range(2):
        mine, theirs = (own, other) if core == 0 else (other, own)
        for p in range(parts):
            tail = jnp.where(first, mine[p, padded - 8 : padded, :].astype(F32), theirs[p, padded - 8 : padded, :].astype(F32))
            meta[p * per : (p + 1) * per, :] = tail[8 - per :, 0:GROUP]
            meta[groups + p * per : groups + (p + 1) * per, :] = tail[8 - per :, GROUP : 2 * GROUP]
        index = meta[0:groups, :]
        scale = jnp.zeros_like(index)
        for entry in range(table.shape[0]):
            scale = jnp.where(index == float(entry), table[entry], scale)
        meta[0:groups, :] = scale
        turned.append(meta[...].T)
    for p in range(parts):
        for core in range(2):
            mine, theirs = (own, other) if core == 0 else (other, own)
            start = (2 * p + core) * rows
            for k in range(per):
                cols = slice(k * GROUP, (k + 1) * GROUP)
                code = jnp.where(first, mine[p, :, cols], theirs[p, :, cols]).astype(F32)
                at = p * per + k
                scale = turned[core][0:padded, at : at + 1]
                width_bits = turned[core][0:padded, groups + at : groups + at + 1]
                two = jnp.floor(code * 0.25) * 4.0 + 2.0
                three = jnp.floor(code * 0.5) * 2.0 + 1.0
                cand = jnp.where(width_bits == 2.0, two, jnp.where(width_bits == 3.0, three, code))
                base_w = ((code - 8.0) * scale).astype(BF16).astype(F32)
                cand_w = ((cand - 8.0) * scale).astype(BF16).astype(F32)
                base_acc[start : start + padded, cols] = base_w
                diff_acc[start : start + padded, cols] = cand_w - base_w
    total = base.shape[0]
    base[...] = base_acc[0:total, :].astype(BF16)
    diff[...] = diff_acc[0:total, :].astype(BF16)


def matmul_kernel(t0, t1, t2, t3, base_w, diff_w, place, out, left, base_acc, diff_acc, both):
    rows = t0.shape[0]
    for k, piece in enumerate((t0, t1, t2, t3)):
        left[k * rows : (k + 1) * rows, :] = piece[...]
    base_acc[...] = jnp.dot(left[...], base_w[...], preferred_element_type=F32)
    diff_acc[...] = jnp.dot(left[...], diff_w[...], preferred_element_type=F32)
    toks = rows // 4
    for kx in range(4):
        for kz in range(4):
            start = kx * rows + kz * toks
            both[0:toks, :] = base_acc[start : start + toks, :]
            both[toks : 2 * toks, :] = diff_acc[start : start + toks, :]
            owner = lax.rem(place[0] - kx + 4, 4) * 4 + lax.rem(place[1] - kz + 4, 4)
            out[owner] = both[...].astype(BF16)


def sum_kernel(parts, base, score, total):
    acc = parts[0].astype(F32)
    for k in range(1, parts.shape[0]):
        acc = acc + parts[k].astype(F32)
    total[...] = acc
    toks = acc.shape[0] // 2
    half = acc.shape[1] // 2
    base[0] = total[0:toks, 0:half].astype(BF16)
    base[1] = total[0:toks, half:].astype(BF16)
    gap = total[toks : 2 * toks, :]
    score[...] = jnp.broadcast_to(jnp.sum(gap * gap, axis=1, keepdims=True), score.shape)


def shift(value, axis, by, size=4):
    return lax.ppermute(value, axis, [(i, (i + by) % size) for i in range(size)])


def trade(value, axis, bit, size=4):
    return lax.ppermute(value, axis, [(i, i ^ bit) for i in range(size)])


def local(activations, weight_codes, scale_index, scale_table, bit_widths):
  place = jnp.stack([lax.axis_index(a) for a in ("x", "zh", "c")]).astype(jnp.int32)
  toks, feat = activations.shape
  store, width = weight_codes.shape
  part = width // 16
  padded = store + 4
  wire = call(
      pack_kernel, jax.ShapeDtypeStruct((16, padded, part), BF16), [VMEM] * 3,
      [pltpu.VMEM((128, 128), F32), pltpu.VMEM((128, 128), F32), pltpu.VMEM((padded, part), F32)],
      0, store * width * 6,
  )(weight_codes, scale_index, bit_widths.reshape(store, -1))
  home = lax.all_to_all(wire, ("x", "zh"), 0, 0, tiled=True)
  other = trade(home, "c", 1, 2)

  value = call(
      block_kernel, jax.ShapeDtypeStruct((toks, feat), F32), [VMEM] * 2,
      (), 2 * toks * feat * HB, toks * feat * 6,
  )(activations, sylvester(HB).astype(BF16))
  for axis, bit in (("y", 1), ("y", 2), ("zl", 1), ("zl", 2)):
      sign = jnp.where(lax.axis_index(axis) & bit, -1.0, 1.0).astype(F32)
      value = trade(value, axis, bit) + sign * value
  rotated = (value * (1.0 / math.sqrt(HB * 16))).astype(BF16)
  near = [rotated] + [shift(rotated, "zh", k) for k in (1, 2, 3)]
  mid = jnp.concatenate(near, axis=0)
  far = [mid] + [shift(mid, "x", k) for k in (1, 2, 3)]

  rows = store
  base_w, diff_w = call(
      lambda *refs: weight_kernel(rows, *refs),
      [jax.ShapeDtypeStruct((feat, part), BF16)] * 2, [VMEM, VMEM, SMEM, SMEM],
      [pltpu.VMEM((128, 128), F32)] + [pltpu.VMEM((feat + 8, part), F32)] * 2,
      feat * part * 20, feat * part * 6,
  )(home, other, scale_table, place)
  sums = call(
      matmul_kernel, jax.ShapeDtypeStruct((16, 2 * toks, part), BF16),
      [VMEM] * 6 + [SMEM],
      [pltpu.VMEM((16 * toks, feat), BF16)] + [pltpu.VMEM((16 * toks, part), F32)] * 2
      + [pltpu.VMEM((2 * toks, part), F32)],
      4 * 16 * toks * feat * part, feat * part * 4 + 16 * toks * feat * 2,
  )(*far, base_w, diff_w, place)
  gathered = lax.all_to_all(sums, ("zl", "y"), 0, 0, tiled=True)
  halves, score = call(
      sum_kernel,
      [jax.ShapeDtypeStruct((2, toks, part // 2), BF16), jax.ShapeDtypeStruct((toks, 128), F32)],
      [VMEM], [pltpu.VMEM((2 * toks, part), F32)], 16 * 40 * part, 16 * 80 * part,
  )(gathered)
  spread = jnp.broadcast_to(score[:, 0][None, None, :], (32, 1, toks))
  everyone = lax.all_to_all(spread, ("x", "zh", "c"), 0, 0, tiled=True)
  scores = jnp.sum(everyone.reshape(16, 2 * toks), axis=0)[None] / SCORE_DIVISOR
  core = lax.axis_index("c")
  keep = lax.dynamic_index_in_dim(halves, core, 0, False)
  send = lax.dynamic_index_in_dim(halves, 1 - core, 0, False)
  got = trade(send, "c", 1, 2)
  base = jnp.where(core == 0, jnp.concatenate([keep, got], 0), jnp.concatenate([got, keep], 0))
  return base, scores


def solution(mesh):
    fine = Mesh(mesh.devices.reshape(SIZES), AXES)
    dp, tensor = ("x", "zh", "c"), ("zl", "y")
    return jax.shard_map(
        local, mesh=fine,
        in_specs=(P(dp, tensor), P(tensor + dp, None), P(tensor + dp, None), P(), P(None, tensor + dp, None)),
        out_specs=(P(tensor, dp), P(None, tensor)),
        check_vma=False,
    )
```

```python
import math

import jax
import jax.numpy as jnp
import numpy as np
from jax import lax
from jax.experimental import pallas as pl
from jax.experimental.pallas import tpu as pltpu
from jax.sharding import Mesh, PartitionSpec as P


HB = 128
LANES = 128
AXES = ("x", "zh", "c", "zl", "y")
SIZES = (4, 4, 2, 4, 4)
CHUNK = 104
SCORE_DIVISOR = 512.0
F32 = jnp.float32
BF16 = jnp.bfloat16
VMEM = pl.BlockSpec(memory_space=pltpu.VMEM)
SMEM = pl.BlockSpec(memory_space=pltpu.SMEM)


def chunk_signs():
    at = np.arange(HB)
    both = at[:, None] & at[None, :]
    parity = np.zeros((HB, HB), np.int64)
    for bit in range(7):
        parity ^= both >> bit & 1
    block = 1 - 2 * parity
    signs = np.zeros((16, 2 * HB, LANES), np.float32)
    first = []
    for m in range(16):
        n0 = min(CHUNK * m // HB, 11)
        first.append(n0 * HB)
        for w in range(CHUNK):
            h = CHUNK * m + w
            row = (h // HB - n0) * HB
            signs[m, row : row + HB, w] = block[:, h % HB]
    return signs, first


SIGNS, FIRST = chunk_signs()


def call(kernel, out_shape, in_specs, scratch=(), flops=0, moved=0, limit=16):
    multi = isinstance(out_shape, (list, tuple))
    return pl.pallas_call(
        kernel,
        out_shape=out_shape,
        in_specs=in_specs,
        out_specs=[VMEM] * len(out_shape) if multi else VMEM,
        scratch_shapes=list(scratch),
        compiler_params=pltpu.CompilerParams(vmem_limit_bytes=limit << 20),
        cost_estimate=pl.CostEstimate(flops=flops, bytes_accessed=moved, transcendentals=0),
    )


def block_kernel(act, signs, out):
    for m in range(16):
        xd, zd = divmod(m, 4)
        piece = jnp.dot(act[:, FIRST[m] : FIRST[m] + 2 * HB], signs[m], preferred_element_type=F32)
        out[zd, :, xd * LANES : (xd + 1) * LANES] = piece


def pack_kernel(codes, index, bits, out, meta, turned, block):
    rows = codes.shape[0]
    groups = index.shape[1]
    meta[...] = jnp.zeros_like(meta)
    meta[0:rows, 0:groups] = index[...].astype(F32)
    meta[0:rows, groups : 2 * groups] = bits[...].astype(F32)
    turned[...] = meta[...].T
    block[...] = jnp.zeros_like(block)
    for p in range(16):
        xd, yd = divmod(p, 4)
        for k in range(4):
            g = 16 * xd + 4 * k + yd
            block[0:rows, k * LANES : (k + 1) * LANES] = codes[:, g * LANES : (g + 1) * LANES].astype(F32)
            block[rows + k : rows + k + 1, 0:LANES] = turned[g : g + 1, :]
            block[rows + k : rows + k + 1, LANES : 2 * LANES] = turned[groups + g : groups + g + 1, :]
        out[p] = block[...].astype(BF16)


def weight_kernel(rows, own, other, table, place, base, diff, meta, base_acc, diff_acc):
    padded = own.shape[1]
    first = place[2] == 0
    turned = []
    for core in range(2):
        mine, theirs = (own, other) if core == 0 else (other, own)
        for p in range(16):
            tail = jnp.where(first, mine[p, padded - 8 : padded, :].astype(F32), theirs[p, padded - 8 : padded, :].astype(F32))
            meta[p * 4 : p * 4 + 4, :] = tail[4:, 0:LANES]
            meta[64 + p * 4 : 68 + p * 4, :] = tail[4:, LANES : 2 * LANES]
        index = meta[0:64, :]
        scale = jnp.zeros_like(index)
        for entry in range(table.shape[0]):
            scale = jnp.where(index == float(entry), table[entry], scale)
        meta[0:64, :] = scale
        turned.append(meta[...].T)
    blank = jnp.zeros((LANES - 2 * rows, own.shape[2]), F32)
    for yd in range(4):
        for xd in range(4):
            p = xd * 4 + yd
            top = (yd * 4 + xd) * LANES
            for core in range(2):
                mine, theirs = (own, other) if core == 0 else (other, own)
                start = top + core * rows
                for k in range(4):
                    cols = slice(k * LANES, (k + 1) * LANES)
                    code = jnp.where(first, mine[p, :, cols], theirs[p, :, cols]).astype(F32)
                    at = p * 4 + k
                    scale = turned[core][0:padded, at : at + 1]
                    held = turned[core][0:padded, 64 + at : 65 + at]
                    two = jnp.floor(code * 0.25) * 4.0 + 2.0
                    three = jnp.floor(code * 0.5) * 2.0 + 1.0
                    cand = jnp.where(held == 2.0, two, jnp.where(held == 3.0, three, code))
                    base_w = ((code - 8.0) * scale).astype(BF16).astype(F32)
                    cand_w = ((cand - 8.0) * scale).astype(BF16).astype(F32)
                    base_acc[start : start + padded, cols] = base_w
                    diff_acc[start : start + padded, cols] = cand_w - base_w
            base_acc[top + 2 * rows : top + LANES, :] = blank
            diff_acc[top + 2 * rows : top + LANES, :] = blank
    base[...] = base_acc[...].astype(BF16)
    diff[...] = diff_acc[...].astype(BF16)


def matmul_kernel(tokens, base_w, diff_w, out, left):
    rows, wide = tokens.shape[1:]
    factor = 1.0 / math.sqrt(HB * 16)
    for xd in range(4):
        s = [tokens[xd * 4 + yd].astype(F32) for yd in range(4)]
        a, b, c, d = s[0] + s[1], s[0] - s[1], s[2] + s[3], s[2] - s[3]
        for j, mixed in enumerate((a + c, b + d, a - c, b - d)):
            left[xd * rows : (xd + 1) * rows, j * wide : (j + 1) * wide] = (mixed * factor).astype(BF16)
    base = jnp.dot(left[...], base_w[...], preferred_element_type=F32).astype(BF16)
    diff = jnp.dot(left[...], diff_w[...], preferred_element_type=F32).astype(BF16)
    for xd in range(4):
        out[xd, 0:rows, :] = base[xd * rows : (xd + 1) * rows, :]
        out[xd, rows : 2 * rows, :] = diff[xd * rows : (xd + 1) * rows, :]


def near_kernel(parts, out, base, send):
    rows = parts.shape[1] // 2
    toks = rows // 4
    total = parts[0].astype(F32)
    for k in range(1, 4):
        total = total + parts[k].astype(F32)
    base[...] = total[0:rows, :]
    for zd in range(4):
        send[0:rows, :] = total[rows:, :]
        for yd in range(4):
            send[rows : rows + toks, yd * LANES : (yd + 1) * LANES] = base[
                yd * toks : (yd + 1) * toks, zd * LANES : (zd + 1) * LANES
            ]
        out[zd] = send[...].astype(BF16)


def far_kernel(parts, base, score, total):
    acc = parts[0].astype(F32)
    for k in range(1, 4):
        acc = acc + parts[k].astype(F32)
    total[...] = acc
    rows = score.shape[0]
    toks = rows // 4
    for yd in range(4):
        base[yd] = total[rows : rows + toks, yd * LANES : (yd + 1) * LANES].astype(BF16)
    gap = total[0:rows, :]
    score[...] = jnp.broadcast_to(jnp.sum(gap * gap, axis=1, keepdims=True), score.shape)


def trade(value, axis, bit, size=4):
    return lax.ppermute(value, axis, [(i, i ^ bit) for i in range(size)])


def local(activations, weight_codes, scale_index, scale_table, bit_widths):
  place = jnp.stack([lax.axis_index(a) for a in ("x", "zh", "c", "y")]).astype(jnp.int32)
  toks, feat = activations.shape
  store, width = weight_codes.shape
  part = width // 16
  padded = store + 4
  wire = call(
      pack_kernel, jax.ShapeDtypeStruct((16, padded, part), BF16), [VMEM] * 3,
      [pltpu.VMEM((128, 128), F32), pltpu.VMEM((128, 128), F32), pltpu.VMEM((padded, part), F32)],
      0, store * width * 6, 8,
  )(weight_codes, scale_index, bit_widths.reshape(store, -1))
  home = lax.all_to_all(wire, ("x", "y"), 0, 0, tiled=True)
  other = trade(home, "c", 1, 2)

  value = call(
      block_kernel, jax.ShapeDtypeStruct((4, toks, 4 * LANES), F32), [VMEM] * 2,
      (), 2 * toks * 4096 * HB, 1 << 20, 8,
  )(activations, jnp.asarray(SIGNS, BF16))
  for axis, bit in (("zl", 1), ("zl", 2)):
      sign = jnp.where(lax.axis_index(axis) & bit, -1.0, 1.0).astype(F32)
      value = trade(value, axis, bit) + sign * value
  value = lax.all_to_all(value.astype(BF16), "zh", 0, 0, tiled=True)
  value = value.reshape(4 * toks, 4 * LANES)
  tokens = lax.all_to_all(jnp.broadcast_to(value[None], (16,) + value.shape), ("x", "y"), 0, 0, tiled=True)

  base_w, diff_w = call(
      lambda *refs: weight_kernel(store, *refs),
      [jax.ShapeDtypeStruct((16 * LANES, part), BF16)] * 2, [VMEM, VMEM, SMEM, SMEM],
      [pltpu.VMEM((128, 128), F32)] + [pltpu.VMEM((16 * LANES, part), F32)] * 2,
      feat * part * 20, feat * part * 6, 24,
  )(home, other, scale_table, place)
  sums = call(
      matmul_kernel, jax.ShapeDtypeStruct((4, 8 * toks, part), BF16),
      [VMEM] * 3, [pltpu.VMEM((16 * toks, 16 * LANES), BF16)],
      4 * 16 * toks * feat * part, feat * part * 4 + 16 * toks * feat * 2, 20,
  )(tokens, base_w, diff_w)
  near = lax.all_to_all(sums, "zl", 0, 0, tiled=True)
  wave = call(
      near_kernel, jax.ShapeDtypeStruct((4, 5 * toks, part), BF16), [VMEM],
      [pltpu.VMEM((4 * toks, part), F32), pltpu.VMEM((5 * toks, part), F32)],
      32 * toks * part, 64 * toks * part, 8,
  )(near)
  far = lax.all_to_all(wave, "zh", 0, 0, tiled=True)
  pieces, score = call(
      far_kernel,
      [jax.ShapeDtypeStruct((4, toks, LANES), BF16), jax.ShapeDtypeStruct((4 * toks, LANES), F32)],
      [VMEM], [pltpu.VMEM((5 * toks, part), F32)], 32 * toks * part, 40 * toks * part, 8,
  )(far)
  mine = score[:, 0].reshape(1, 4, 1, 1, toks)
  spread = jnp.broadcast_to(mine, (4, 4, 2, 1, toks)).reshape(32, 1, toks)
  everyone = lax.all_to_all(spread, ("x", "y", "c"), 0, 0, tiled=True)
  scores = jnp.sum(everyone.reshape(16, 2 * toks), axis=0)[None] / SCORE_DIVISOR
  y, c = lax.axis_index("y"), lax.axis_index("c")
  got = []
  for r in range(4):
      pairs = []
      for cs in range(2):
          for ys in range(4):
              pairs.append((cs * 4 + ys, (ys // 2) * 4 + (2 * (ys % 2) + cs + r) % 4))
      piece = lax.dynamic_index_in_dim(pieces, lax.rem(2 * lax.rem(y, 2) + c + r, 4), 0, False)
      got.append(lax.ppermute(piece, ("c", "y"), pairs))
  got = jnp.stack(got)
  rows = []
  for cs in range(2):
      rows.append(jnp.concatenate(
          [lax.dynamic_index_in_dim(got, lax.rem(y - 2 * i - cs + 4, 4), 0, False) for i in range(2)], axis=1))
  base = jnp.concatenate(rows, axis=0)
  return base, scores


def solution(mesh):
    fine = Mesh(mesh.devices.reshape(SIZES), AXES)
    dp, tensor = ("x", "zh", "c"), ("zl", "y")
    return jax.shard_map(
        local, mesh=fine,
        in_specs=(P(dp, tensor), P(tensor + dp, None), P(tensor + dp, None), P(), P(None, tensor + dp, None)),
        out_specs=(P(tensor, dp), P(None, tensor)),
        check_vma=False,
    )
```

```python
import math

import jax
import jax.numpy as jnp
import numpy as np
from jax import lax
from jax.experimental import pallas as pl
from jax.experimental.pallas import tpu as pltpu
from jax.sharding import Mesh, PartitionSpec as P


HB = 128
LANES = 128
AXES = ("x", "zh", "c", "zl", "y")
SIZES = (4, 4, 2, 4, 4)
CHUNK = 104
SCORE_DIVISOR = 512.0
F32 = jnp.float32
BF16 = jnp.bfloat16
VMEM = pl.BlockSpec(memory_space=pltpu.VMEM)
SMEM = pl.BlockSpec(memory_space=pltpu.SMEM)


def chunk_signs():
    at = np.arange(HB)
    both = at[:, None] & at[None, :]
    parity = np.zeros((HB, HB), np.int64)
    for bit in range(7):
        parity ^= both >> bit & 1
    block = 1 - 2 * parity
    signs = np.zeros((16, 2 * HB, LANES), np.float32)
    first = []
    for m in range(16):
        n0 = min(CHUNK * m // HB, 11)
        first.append(n0 * HB)
        for w in range(CHUNK):
            h = CHUNK * m + w
            row = (h // HB - n0) * HB
            signs[m, row : row + HB, w] = block[:, h % HB]
    return signs, first


SIGNS, FIRST = chunk_signs()


def call(kernel, out_shape, in_specs, scratch=(), flops=0, moved=0, limit=16):
    multi = isinstance(out_shape, (list, tuple))
    return pl.pallas_call(
        kernel,
        out_shape=out_shape,
        in_specs=in_specs,
        out_specs=[VMEM] * len(out_shape) if multi else VMEM,
        scratch_shapes=list(scratch),
        compiler_params=pltpu.CompilerParams(vmem_limit_bytes=limit << 20),
        cost_estimate=pl.CostEstimate(flops=flops, bytes_accessed=moved, transcendentals=0),
    )


def block_kernel(act, signs, out):
    for m in range(16):
        xd, zd = divmod(m, 4)
        piece = jnp.dot(act[:, FIRST[m] : FIRST[m] + 2 * HB], signs[m], preferred_element_type=F32)
        out[zd, :, xd * LANES : (xd + 1) * LANES] = piece


def pack_kernel(codes, index, bits, out, meta, turned, block):
    rows = codes.shape[0]
    groups = index.shape[1]
    xd = pl.program_id(0)

    @pl.when(xd == 0)
    def _():
        meta[...] = jnp.zeros_like(meta)
        meta[0:rows, 0:groups] = index[...].astype(F32)
        meta[0:rows, groups : 2 * groups] = bits[...].astype(F32)
        turned[...] = meta[...].T
        block[...] = jnp.zeros_like(block)

    index_rows = turned[pl.ds(pl.multiple_of(16 * xd, 16), 16), :]
    bits_rows = turned[pl.ds(pl.multiple_of(groups + 16 * xd, 16), 16), :]
    for yd in range(4):
        for k in range(4):
            g = 4 * k + yd
            block[0:rows, k * LANES : (k + 1) * LANES] = codes[:, g * LANES : (g + 1) * LANES].astype(F32)
            block[rows + k : rows + k + 1, 0:LANES] = index_rows[g : g + 1, :]
            block[rows + k : rows + k + 1, LANES : 2 * LANES] = bits_rows[g : g + 1, :]
        out[yd] = block[...].astype(BF16)


def weight_kernel(rows, own, other, table, place, base, diff, meta, base_acc, diff_acc):
    padded = own.shape[1]
    first = place[2] == 0
    turned = []
    for core in range(2):
        mine, theirs = (own, other) if core == 0 else (other, own)
        for p in range(16):
            tail = jnp.where(first, mine[p, padded - 8 : padded, :].astype(F32), theirs[p, padded - 8 : padded, :].astype(F32))
            meta[p * 4 : p * 4 + 4, :] = tail[4:, 0:LANES]
            meta[64 + p * 4 : 68 + p * 4, :] = tail[4:, LANES : 2 * LANES]
        index = meta[0:64, :]
        scale = jnp.zeros_like(index)
        for entry in range(table.shape[0]):
            scale = jnp.where(index == float(entry), table[entry], scale)
        meta[0:64, :] = scale
        turned.append(meta[...].T)
    blank = jnp.zeros((LANES - 2 * rows, own.shape[2]), F32)
    for yd in range(4):
        for xd in range(4):
            p = xd * 4 + yd
            top = (yd * 4 + xd) * LANES
            for core in range(2):
                mine, theirs = (own, other) if core == 0 else (other, own)
                start = top + core * rows
                for k in range(4):
                    cols = slice(k * LANES, (k + 1) * LANES)
                    code = jnp.where(first, mine[p, :, cols], theirs[p, :, cols]).astype(F32)
                    at = p * 4 + k
                    scale = turned[core][0:padded, at : at + 1]
                    held = turned[core][0:padded, 64 + at : 65 + at]
                    two = jnp.floor(code * 0.25) * 4.0 + 2.0
                    three = jnp.floor(code * 0.5) * 2.0 + 1.0
                    cand = jnp.where(held == 2.0, two, jnp.where(held == 3.0, three, code))
                    base_w = ((code - 8.0) * scale).astype(BF16).astype(F32)
                    cand_w = ((cand - 8.0) * scale).astype(BF16).astype(F32)
                    base_acc[start : start + padded, cols] = base_w
                    diff_acc[start : start + padded, cols] = cand_w - base_w
            base_acc[top + 2 * rows : top + LANES, :] = blank
            diff_acc[top + 2 * rows : top + LANES, :] = blank
    base[...] = base_acc[...].astype(BF16)
    diff[...] = diff_acc[...].astype(BF16)


def matmul_kernel(tokens, base_w, diff_w, out, left):
    rows, wide = tokens.shape[1:]
    factor = 1.0 / math.sqrt(HB * 16)
    for xd in range(4):
        s = [tokens[xd * 4 + yd].astype(F32) for yd in range(4)]
        a, b, c, d = s[0] + s[1], s[0] - s[1], s[2] + s[3], s[2] - s[3]
        for j, mixed in enumerate((a + c, b + d, a - c, b - d)):
            left[xd * rows : (xd + 1) * rows, j * wide : (j + 1) * wide] = (mixed * factor).astype(BF16)
    base = jnp.dot(left[...], base_w[...], preferred_element_type=F32).astype(BF16)
    diff = jnp.dot(left[...], diff_w[...], preferred_element_type=F32).astype(BF16)
    for xd in range(4):
        out[xd, 0:rows, :] = base[xd * rows : (xd + 1) * rows, :]
        out[xd, rows : 2 * rows, :] = diff[xd * rows : (xd + 1) * rows, :]


def near_kernel(parts, out, base, send):
    rows = parts.shape[1] // 2
    toks = rows // 4
    total = parts[0].astype(F32)
    for k in range(1, 4):
        total = total + parts[k].astype(F32)
    base[...] = total[0:rows, :]
    for zd in range(4):
        send[0:rows, :] = total[rows:, :]
        for yd in range(4):
            send[rows : rows + toks, yd * LANES : (yd + 1) * LANES] = base[
                yd * toks : (yd + 1) * toks, zd * LANES : (zd + 1) * LANES
            ]
        out[zd] = send[...].astype(BF16)


def far_kernel(parts, out, total, turn, block):
    acc = parts[0].astype(F32)
    for k in range(1, 4):
        acc = acc + parts[k].astype(F32)
    total[...] = acc
    rows = parts.shape[1] * 4 // 5
    toks = rows // 4
    gap = total[0:rows, :]
    turn[rows:, :] = jnp.zeros((LANES - rows, LANES), F32)
    turn[0:rows, :] = jnp.broadcast_to(jnp.sum(gap * gap, axis=1, keepdims=True), (rows, LANES))
    score = turn[...].T[0:1, :]
    high = score.astype(BF16).astype(F32)
    middle = (score - high).astype(BF16).astype(F32)
    low = score - high - middle
    block[toks : toks + 1, :] = high
    block[toks + 1 : toks + 2, :] = middle
    block[toks + 2 : toks + 3, :] = low
    block[toks + 3 : toks + 4, :] = jnp.zeros((1, LANES), F32)
    for yd in range(4):
        block[0:toks, :] = total[rows : rows + toks, yd * LANES : (yd + 1) * LANES]
        wire = block[...].astype(BF16)
        for xd in range(4):
            for cd in range(2):
                out[(xd * 4 + yd) * 2 + cd] = wire


def last_kernel(parts, place, base, score, held):
    toks = parts.shape[1] - 4
    x, c, y = place[0], place[2], place[3]
    lane = lax.broadcasted_iota(jnp.int32, (LANES, LANES), 0)
    slot = lax.broadcasted_iota(jnp.int32, (LANES, LANES), 1)
    final = jnp.zeros((8, LANES), F32)
    for cs in range(2):
        total = jnp.zeros((8, LANES), F32)
        for k in range(16):
            total = total + parts[2 * k + cs, toks - 4 : toks + 4, :].astype(F32)
        row = total[4:5, :] + total[5:6, :] + total[6:7, :]
        pick = jnp.where((lane == y * toks + slot - cs * toks) & (slot >= cs * toks) & (slot < (cs + 1) * toks), 1.0, 0.0)
        final = final + jnp.dot(jnp.broadcast_to(row, (8, LANES)), pick, precision=lax.Precision.HIGHEST, preferred_element_type=F32)
        for i in range(2):
            piece = parts[(x * 4 + 2 * c + i) * 2 + cs]
            held[cs * toks : (cs + 1) * toks, i * LANES : (i + 1) * LANES] = piece[0:toks, :].astype(F32)
    base[...] = held[...].astype(BF16)
    score[...] = final[0:1, 0 : 2 * toks] * (1.0 / SCORE_DIVISOR)


def trade(value, axis, bit, size=4):
    return lax.ppermute(value, axis, [(i, i ^ bit) for i in range(size)])


def local(activations, weight_codes, scale_index, scale_table, bit_widths):
  place = jnp.stack([lax.axis_index(a) for a in ("x", "zh", "c", "y")]).astype(jnp.int32)
  toks, feat = activations.shape
  store, width = weight_codes.shape
  part = width // 16
  padded = store + 4
  whole = lambda i: (0, 0)
  wire = pl.pallas_call(
      pack_kernel, out_shape=jax.ShapeDtypeStruct((16, padded, part), BF16), grid=(4,),
      in_specs=[
          pl.BlockSpec((store, width // 4), lambda i: (0, i)),
          pl.BlockSpec(scale_index.shape, whole),
          pl.BlockSpec(scale_index.shape, whole),
      ],
      out_specs=pl.BlockSpec((4, padded, part), lambda i: (i, 0, 0)),
      scratch_shapes=[pltpu.VMEM((128, 128), F32), pltpu.VMEM((128, 128), F32), pltpu.VMEM((padded, part), F32)],
      name="pack", compiler_params=pltpu.CompilerParams(vmem_limit_bytes=60 << 20),
      cost_estimate=pl.CostEstimate(flops=0, bytes_accessed=store * width * 6, transcendentals=0),
  )(weight_codes, scale_index, bit_widths.reshape(store, -1))
  home = lax.all_to_all(wire, ("x", "y"), 0, 0, tiled=True)
  other = trade(home, "c", 1, 2)

  value = call(
      block_kernel, jax.ShapeDtypeStruct((4, toks, 4 * LANES), F32), [VMEM] * 2,
      (), 2 * toks * 4096 * HB, 1 << 20, 8,
  )(activations, jnp.asarray(SIGNS, BF16))
  for axis, bit in (("zl", 1), ("zl", 2)):
      sign = jnp.where(lax.axis_index(axis) & bit, -1.0, 1.0).astype(F32)
      value = trade(value, axis, bit) + sign * value
  value = lax.all_to_all(value.astype(BF16), "zh", 0, 0, tiled=True)
  value = value.reshape(4 * toks, 4 * LANES)
  tokens = lax.all_to_all(jnp.broadcast_to(value[None], (16,) + value.shape), ("x", "y"), 0, 0, tiled=True)

  base_w, diff_w = call(
      lambda *refs: weight_kernel(store, *refs),
      [jax.ShapeDtypeStruct((16 * LANES, part), BF16)] * 2, [VMEM, VMEM, SMEM, SMEM],
      [pltpu.VMEM((128, 128), F32)] + [pltpu.VMEM((16 * LANES, part), F32)] * 2,
      feat * part * 20, feat * part * 6, 16,
  )(home, other, scale_table, place)
  sums = call(
      matmul_kernel, jax.ShapeDtypeStruct((4, 8 * toks, part), BF16),
      [VMEM] * 3, [pltpu.VMEM((16 * toks, 16 * LANES), BF16)],
      4 * 16 * toks * feat * part, feat * part * 4 + 16 * toks * feat * 2, 10,
  )(tokens, base_w, diff_w)
  near = lax.all_to_all(sums, "zl", 0, 0, tiled=True)
  wave = call(
      near_kernel, jax.ShapeDtypeStruct((4, 5 * toks, part), BF16), [VMEM],
      [pltpu.VMEM((4 * toks, part), F32), pltpu.VMEM((5 * toks, part), F32)],
      32 * toks * part, 64 * toks * part, 8,
  )(near)
  far = lax.all_to_all(wave, "zh", 0, 0, tiled=True)
  wire = call(
      far_kernel, jax.ShapeDtypeStruct((32, toks + 4, LANES), BF16), [VMEM],
      [pltpu.VMEM((5 * toks, part), F32), pltpu.VMEM((LANES, LANES), F32), pltpu.VMEM((toks + 4, LANES), F32)],
      32 * toks * part, 40 * toks * part, 4,
  )(far)
  everyone = lax.all_to_all(wire, ("x", "y", "c"), 0, 0, tiled=True)
  base, scores = call(
      last_kernel,
      [jax.ShapeDtypeStruct((2 * toks, 2 * LANES), BF16), jax.ShapeDtypeStruct((1, 2 * toks), F32)],
      [VMEM, SMEM], [pltpu.VMEM((2 * toks, 2 * LANES), F32)], 1 << 20, 1 << 18, 4,
  )(everyone, place)
  return base, scores


def solution(mesh):
    fine = Mesh(mesh.devices.reshape(SIZES), AXES)
    dp, tensor = ("x", "zh", "c"), ("zl", "y")
    return jax.shard_map(
        local, mesh=fine,
        in_specs=(P(dp, tensor), P(tensor + dp, None), P(tensor + dp, None), P(), P(None, tensor + dp, None)),
        out_specs=(P(tensor, dp), P(None, tensor)),
        check_vma=False,
    )
```

```python
import math

import jax
import jax.numpy as jnp
import numpy as np
from jax import lax
from jax.experimental import pallas as pl
from jax.experimental.pallas import tpu as pltpu
from jax.sharding import Mesh, PartitionSpec as P


HB = 128
LANES = 128
AXES = ("x", "zh", "c", "zl", "y")
SIZES = (4, 4, 2, 4, 4)
CHUNK = 104
SCORE_DIVISOR = 512.0
F32 = jnp.float32
BF16 = jnp.bfloat16
VMEM = pl.BlockSpec(memory_space=pltpu.VMEM)
SMEM = pl.BlockSpec(memory_space=pltpu.SMEM)


def chunk_signs():
    at = np.arange(HB)
    both = at[:, None] & at[None, :]
    parity = np.zeros((HB, HB), np.int64)
    for bit in range(7):
        parity ^= both >> bit & 1
    block = 1 - 2 * parity
    signs = np.zeros((16, 2 * HB, LANES), np.float32)
    first = []
    for m in range(16):
        n0 = min(CHUNK * m // HB, 11)
        first.append(n0 * HB)
        for w in range(CHUNK):
            h = CHUNK * m + w
            row = (h // HB - n0) * HB
            signs[m, row : row + HB, w] = block[:, h % HB]
    return signs, first


SIGNS, FIRST = chunk_signs()


def call(kernel, out_shape, in_specs, scratch=(), flops=0, moved=0, limit=16):
    multi = isinstance(out_shape, (list, tuple))
    return pl.pallas_call(
        kernel,
        out_shape=out_shape,
        in_specs=in_specs,
        out_specs=[VMEM] * len(out_shape) if multi else VMEM,
        scratch_shapes=list(scratch),
        compiler_params=pltpu.CompilerParams(vmem_limit_bytes=limit << 20),
        cost_estimate=pl.CostEstimate(flops=flops, bytes_accessed=moved, transcendentals=0),
    )


def block_kernel(act, signs, out):
    for m in range(16):
        xd, zd = divmod(m, 4)
        piece = jnp.dot(act[:, FIRST[m] : FIRST[m] + 2 * HB], signs[m], preferred_element_type=F32)
        out[zd, :, xd * LANES : (xd + 1) * LANES] = piece.astype(BF16)


def pack_kernel(codes_hbm, index, bits, out, codes, meta, turned, block, sems):
    rows, width = codes.shape
    quarter = width // 4
    groups = index.shape[1]
    copies = []
    for xd in range(4):
        cols = pl.ds(xd * quarter, quarter)
        copies.append(pltpu.make_async_copy(codes_hbm.at[:, cols], codes.at[:, cols], sems.at[xd]))
        copies[-1].start()
    meta[...] = jnp.zeros_like(meta)
    meta[0:rows, 0:groups] = index[...].astype(F32)
    meta[0:rows, groups : 2 * groups] = bits[:, 0, :].astype(F32)
    turned[...] = meta[...].T
    block[...] = jnp.zeros_like(block)
    for xd in range(4):
        copies[xd].wait()
        for yd in range(4):
            for k in range(4):
                g = 16 * xd + 4 * k + yd
                block[0:rows, k * LANES : (k + 1) * LANES] = codes[:, g * LANES : (g + 1) * LANES].astype(F32)
                block[rows + k : rows + k + 1, 0:LANES] = turned[g : g + 1, :]
                block[rows + k : rows + k + 1, LANES : 2 * LANES] = turned[groups + g : groups + g + 1, :]
            out[xd * 4 + yd] = block[...].astype(BF16)


def weight_kernel(rows, own, other, table, place, base, diff, meta, base_acc, diff_acc):
    padded = own.shape[1]
    first = place[2] == 0
    turned = []
    for core in range(2):
        mine, theirs = (own, other) if core == 0 else (other, own)
        for p in range(16):
            tail = jnp.where(first, mine[p, padded - 8 : padded, :].astype(F32), theirs[p, padded - 8 : padded, :].astype(F32))
            meta[p * 4 : p * 4 + 4, :] = tail[4:, 0:LANES]
            meta[64 + p * 4 : 68 + p * 4, :] = tail[4:, LANES : 2 * LANES]
        index = meta[0:64, :]
        scale = jnp.zeros_like(index)
        for entry in range(table.shape[0]):
            scale = jnp.where(index == float(entry), table[entry], scale)
        meta[0:64, :] = scale
        turned.append(meta[...].T)
    blank = jnp.zeros((LANES - 2 * rows, own.shape[2]), F32)
    for yd in range(4):
        for xd in range(4):
            p = xd * 4 + yd
            top = (yd * 4 + xd) * LANES
            for core in range(2):
                mine, theirs = (own, other) if core == 0 else (other, own)
                start = top + core * rows
                for k in range(4):
                    cols = slice(k * LANES, (k + 1) * LANES)
                    code = jnp.where(first, mine[p, :, cols], theirs[p, :, cols]).astype(F32)
                    at = p * 4 + k
                    scale = turned[core][0:padded, at : at + 1]
                    held = turned[core][0:padded, 64 + at : 65 + at]
                    two = jnp.floor(code * 0.25) * 4.0 + 2.0
                    three = jnp.floor(code * 0.5) * 2.0 + 1.0
                    cand = jnp.where(held == 2.0, two, jnp.where(held == 3.0, three, code))
                    base_w = ((code - 8.0) * scale).astype(BF16).astype(F32)
                    cand_w = ((cand - 8.0) * scale).astype(BF16).astype(F32)
                    base_acc[start : start + padded, cols] = base_w
                    diff_acc[start : start + padded, cols] = cand_w - base_w
            base_acc[top + 2 * rows : top + LANES, :] = blank
            diff_acc[top + 2 * rows : top + LANES, :] = blank
    base[...] = base_acc[...].astype(BF16)
    diff[...] = diff_acc[...].astype(BF16)


def matmul_kernel(tokens, base_hbm, diff_hbm, out, left, base_w, diff_w, sems):
    rows, wide = tokens.shape[1:]
    copies = [
        pltpu.make_async_copy(base_hbm, base_w, sems.at[0]),
        pltpu.make_async_copy(diff_hbm, diff_w, sems.at[1]),
    ]
    for copy in copies:
        copy.start()
    factor = 1.0 / math.sqrt(HB * 16)
    for xd in range(4):
        s = [tokens[xd * 4 + yd].astype(F32) for yd in range(4)]
        a, b, c, d = s[0] + s[1], s[0] - s[1], s[2] + s[3], s[2] - s[3]
        for j, mixed in enumerate((a + c, b + d, a - c, b - d)):
            left[xd * rows : (xd + 1) * rows, j * wide : (j + 1) * wide] = (mixed * factor).astype(BF16)
    copies[0].wait()
    base = jnp.dot(left[...], base_w[...], preferred_element_type=F32).astype(BF16)
    copies[1].wait()
    diff = jnp.dot(left[...], diff_w[...], preferred_element_type=F32).astype(BF16)
    for xd in range(4):
        out[xd, 0:rows, :] = base[xd * rows : (xd + 1) * rows, :]
        out[xd, rows : 2 * rows, :] = diff[xd * rows : (xd + 1) * rows, :]


def unpad_kernel(parts, out):
    toks = parts.shape[1]
    for k in range(4):
        out[k * toks : (k + 1) * toks, :] = parts[k].astype(F32)


def spread_kernel(got, value, sign, out):
    mixed = (got[...] + sign[0] * value[...]).astype(BF16)
    for k in range(out.shape[0]):
        out[k] = mixed


def near_kernel(parts, out):
    total = parts[0].astype(F32)
    for k in range(1, 4):
        total = total + parts[k].astype(F32)
    for zd in range(4):
        out[zd] = total[:, zd * LANES : (zd + 1) * LANES].astype(BF16)


def far_kernel(parts, place, p0, p1, p2, p3, score, total, turn, pieces):
    acc = parts[0].astype(F32)
    for k in range(1, 4):
        acc = acc + parts[k].astype(F32)
    total[...] = acc
    rows = parts.shape[1] // 2
    toks = rows // 4
    gap = total[rows:, :]
    turn[rows:, :] = jnp.zeros((LANES - rows, LANES), F32)
    turn[0:rows, :] = jnp.broadcast_to(jnp.sum(gap * gap, axis=1, keepdims=True), (rows, LANES))
    line = turn[...].T[0:1, :]
    for k in range(score.shape[0]):
        score[k] = line
    for yd in range(4):
        pieces[yd] = total[yd * toks : (yd + 1) * toks, :]
    first = 2 * lax.rem(place[3], 2) + place[2]
    for r, out in enumerate((p0, p1, p2, p3)):
        out[...] = pieces[lax.rem(first + r, 4)].astype(BF16)


def last_kernel(lines, g0, g1, g2, g3, place, base, score, pieces, held):
    toks = g0.shape[0]
    y = place[3]
    lane = lax.broadcasted_iota(jnp.int32, (LANES, LANES), 0)
    slot = lax.broadcasted_iota(jnp.int32, (LANES, LANES), 1)
    for r, got in enumerate((g0, g1, g2, g3)):
        pieces[r] = got[...].astype(F32)
    final = jnp.zeros((8, LANES), F32)
    for cs in range(2):
        row = jnp.zeros((1, LANES), F32)
        for k in range(16):
            for ys in range(4):
                row = row + lines[(2 * k + cs) * 4 + ys]
        pick = jnp.where((lane == y * toks + slot - cs * toks) & (slot >= cs * toks) & (slot < (cs + 1) * toks), 1.0, 0.0)
        final = final + jnp.dot(jnp.broadcast_to(row, (8, LANES)), pick, precision=lax.Precision.HIGHEST, preferred_element_type=F32)
        for i in range(2):
            held[cs * toks : (cs + 1) * toks, i * LANES : (i + 1) * LANES] = pieces[lax.rem(y - 2 * i - cs + 4, 4)]
    base[...] = held[...].astype(BF16)
    score[...] = final[0:1, 0 : 2 * toks] * (1.0 / SCORE_DIVISOR)


def trade(value, axis, bit, size=4):
    return lax.ppermute(value, axis, [(i, i ^ bit) for i in range(size)])


def local(activations, weight_codes, scale_index, scale_table, bit_widths):
  place = jnp.stack([lax.axis_index(a) for a in ("x", "zh", "c", "y")]).astype(jnp.int32)
  toks, feat = activations.shape
  store, width = weight_codes.shape
  part = width // 16
  padded = store + 4
  wire = call(
      pack_kernel, jax.ShapeDtypeStruct((16, padded, part), BF16),
      [pl.BlockSpec(memory_space=pl.ANY), VMEM, VMEM],
      [pltpu.VMEM((store, width), jnp.int32), pltpu.VMEM((128, 128), F32), pltpu.VMEM((128, 128), F32),
       pltpu.VMEM((padded, part), F32), pltpu.SemaphoreType.DMA((4,))],
      0, store * width * 6, 60,
  )(weight_codes, scale_index, bit_widths.reshape(store, 1, -1))
  home = lax.all_to_all(wire, ("x", "y"), 0, 0, tiled=True)
  other = trade(home, "c", 1, 2)

  value = call(
      block_kernel, jax.ShapeDtypeStruct((4, toks, 4 * LANES), BF16), [VMEM] * 2,
      (), 2 * toks * 4096 * HB, 1 << 20, 8,
  )(activations, jnp.asarray(SIGNS, BF16))
  value = lax.all_to_all(value, "zh", 0, 0, tiled=True)
  value = call(unpad_kernel, jax.ShapeDtypeStruct((4 * toks, 4 * LANES), F32), [VMEM], (), 0, 1 << 18, 4)(value)
  sign = jnp.where(lax.axis_index("zl") & 1, -1.0, 1.0).astype(F32)
  value = trade(value, "zl", 1) + sign * value
  got = trade(value, "zl", 2)
  sign = jnp.where(lax.axis_index("zl") & 2, -1.0, 1.0).astype(F32).reshape(1)
  value = call(
      spread_kernel, jax.ShapeDtypeStruct((16,) + value.shape, BF16), [VMEM, VMEM, SMEM], (), 0, 1 << 21, 8,
  )(got, value, sign)
  tokens = lax.all_to_all(value, ("x", "y"), 0, 0, tiled=True)

  base_w, diff_w = call(
      lambda *refs: weight_kernel(store, *refs),
      [jax.ShapeDtypeStruct((16 * LANES, part), BF16)] * 2, [VMEM, VMEM, SMEM, SMEM],
      [pltpu.VMEM((128, 128), F32)] + [pltpu.VMEM((16 * LANES, part), F32)] * 2,
      feat * part * 20, feat * part * 6, 16,
  )(home, other, scale_table, place)
  sums = call(
      matmul_kernel, jax.ShapeDtypeStruct((4, 8 * toks, part), BF16),
      [VMEM] + [pl.BlockSpec(memory_space=pl.ANY)] * 2,
      [pltpu.VMEM((16 * toks, 16 * LANES), BF16)] + [pltpu.VMEM((16 * LANES, part), BF16)] * 2
      + [pltpu.SemaphoreType.DMA((2,))],
      4 * 16 * toks * feat * part, feat * part * 4 + 16 * toks * feat * 2, 58,
  )(tokens, base_w, diff_w)
  near = lax.all_to_all(sums, "zl", 0, 0, tiled=True)
  wave = call(
      near_kernel, jax.ShapeDtypeStruct((4, 8 * toks, LANES), BF16), [VMEM], (),
      32 * toks * part, 64 * toks * part, 8,
  )(near)
  far = lax.all_to_all(wave, "zh", 0, 0, tiled=True)
  *pieces, line = call(
      far_kernel,
      [jax.ShapeDtypeStruct((toks, LANES), BF16)] * 4 + [jax.ShapeDtypeStruct((128, 1, LANES), F32)],
      [VMEM, SMEM],
      [pltpu.VMEM((8 * toks, LANES), F32), pltpu.VMEM((LANES, LANES), F32), pltpu.VMEM((4, toks, LANES), F32)],
      32 * toks * part, 40 * toks * part, 4,
  )(far, place)
  lines = lax.all_to_all(line, ("x", "zh", "c", "y"), 0, 0, tiled=True)
  got = []
  for r, piece in enumerate(pieces):
      pairs = [
          (cs * 4 + ys, (ys // 2) * 4 + (2 * (ys % 2) + cs + r) % 4) for cs in range(2) for ys in range(4)
      ]
      got.append(lax.ppermute(piece, ("c", "y"), pairs))
  base, scores = call(
      last_kernel,
      [jax.ShapeDtypeStruct((2 * toks, 2 * LANES), BF16), jax.ShapeDtypeStruct((1, 2 * toks), F32)],
      [VMEM] * 5 + [SMEM],
      [pltpu.VMEM((4, toks, LANES), F32), pltpu.VMEM((2 * toks, 2 * LANES), F32)], 1 << 20, 1 << 18, 4,
  )(lines, *got, place)
  return base, scores


def solution(mesh):
    fine = Mesh(mesh.devices.reshape(SIZES), AXES)
    dp, tensor = ("x", "zh", "c"), ("zl", "y")
    return jax.shard_map(
        local, mesh=fine,
        in_specs=(P(dp, tensor), P(tensor + dp, None), P(tensor + dp, None), P(), P(None, tensor + dp, None)),
        out_specs=(P(tensor, dp), P(None, tensor)),
        check_vma=False,
    )
```

```python
import math

import jax
import jax.numpy as jnp
import numpy as np
from jax import lax
from jax.experimental import pallas as pl
from jax.experimental.pallas import tpu as pltpu
from jax.sharding import Mesh, PartitionSpec as P


HB = 128
LANES = 128
AXES = ("x", "zh", "c", "zl", "y")
SIZES = (4, 4, 2, 4, 4)
CHUNK = 104
SCORE_DIVISOR = 512.0
F32 = jnp.float32
BF16 = jnp.bfloat16
VMEM = pl.BlockSpec(memory_space=pltpu.VMEM)
SMEM = pl.BlockSpec(memory_space=pltpu.SMEM)
HBM = pl.BlockSpec(memory_space=pltpu.HBM)


def block_signs():
    at = np.arange(HB)
    both = at[:, None] & at[None, :]
    parity = np.zeros((HB, HB), np.int64)
    for bit in range(7):
        parity ^= both >> bit & 1
    return (1 - 2 * parity).astype(np.float32)


SIGNS = block_signs()


def call(kernel, out_shape, in_specs, scratch=(), flops=0, moved=0, limit=16):
    multi = isinstance(out_shape, (list, tuple))
    return pl.pallas_call(
        kernel,
        out_shape=out_shape,
        in_specs=in_specs,
        out_specs=[VMEM] * len(out_shape) if multi else VMEM,
        scratch_shapes=list(scratch),
        compiler_params=pltpu.CompilerParams(vmem_limit_bytes=int(limit * (1 << 20))),
        cost_estimate=pl.CostEstimate(flops=flops, bytes_accessed=moved, transcendentals=0),
    )


def block_kernel(act, signs, out, work):
    toks = act.shape[0]
    blocks = act.shape[1] // HB
    for n in range(blocks):
        work[n, 0:toks, :] = jnp.dot(act[:, n * HB : (n + 1) * HB], signs[...], preferred_element_type=F32)
    lane = lax.broadcasted_iota(jnp.int32, work.shape[1:], 1)
    for m in range(16):
        xd, zd = divmod(m, 4)
        n, offset = divmod(CHUNK * m, HB)
        piece = work[n]
        if offset:
            piece = pltpu.roll(piece, HB - offset, 1)
            if offset + CHUNK > HB:
                piece = jnp.where(lane < HB - offset, piece, pltpu.roll(work[n + 1], HB - offset, 1))
        piece = jnp.where(lane < CHUNK, piece, 0.0)
        out[zd, :, xd * LANES : (xd + 1) * LANES] = piece[0:toks, :].astype(BF16)


def pack_kernel(codes_hbm, index, bits, out, codes, meta, turned, block, sems):
    rows, width = codes.shape
    quarter = width // 4
    groups = index.shape[1]
    copies = []
    for xd in range(4):
        cols = pl.ds(xd * quarter, quarter)
        copies.append(pltpu.make_async_copy(codes_hbm.at[:, cols], codes.at[:, cols], sems.at[xd]))
        copies[-1].start()
    meta[...] = jnp.zeros_like(meta)
    meta[0:rows, 0:groups] = index[...].astype(F32)
    meta[0:rows, groups : 2 * groups] = bits[:, 0, :].astype(F32)
    turned[...] = meta[...].T
    block[...] = jnp.zeros_like(block)
    for xd in range(4):
        copies[xd].wait()
        for yd in range(4):
            for k in range(4):
                g = 16 * xd + 4 * k + yd
                block[0:rows, k * LANES : (k + 1) * LANES] = codes[:, g * LANES : (g + 1) * LANES].astype(F32)
                block[rows + k : rows + k + 1, 0:LANES] = turned[g : g + 1, :]
                block[rows + k : rows + k + 1, LANES : 2 * LANES] = turned[groups + g : groups + g + 1, :]
            out[xd * 4 + yd] = block[...].astype(BF16)


def weight_kernel(rows, own, other, table, place, base_hbm, diff_hbm, meta, base_acc, diff_acc, base, diff, sems):
    padded = own.shape[1]
    first = place[2] == 0
    turned = []
    for core in range(2):
        mine, theirs = (own, other) if core == 0 else (other, own)
        for p in range(16):
            tail = jnp.where(first, mine[p, padded - 8 : padded, :].astype(F32), theirs[p, padded - 8 : padded, :].astype(F32))
            meta[p * 4 : p * 4 + 4, :] = tail[4:, 0:LANES]
            meta[64 + p * 4 : 68 + p * 4, :] = tail[4:, LANES : 2 * LANES]
        index = meta[0:64, :]
        scale = jnp.zeros_like(index)
        for entry in range(table.shape[0]):
            scale = jnp.where(index == float(entry), table[entry], scale)
        meta[0:64, :] = scale
        turned.append(meta[...].T)
    blank = jnp.zeros((LANES - 2 * rows, own.shape[2]), F32)
    copies = []
    for yd in range(4):
        for xd in range(4):
            p = xd * 4 + yd
            top = (yd * 4 + xd) * LANES
            for core in range(2):
                mine, theirs = (own, other) if core == 0 else (other, own)
                start = top + core * rows
                for k in range(4):
                    cols = slice(k * LANES, (k + 1) * LANES)
                    code = jnp.where(first, mine[p, :, cols], theirs[p, :, cols]).astype(F32)
                    at = p * 4 + k
                    scale = turned[core][0:padded, at : at + 1]
                    held = turned[core][0:padded, 64 + at : 65 + at]
                    two = jnp.floor(code * 0.25) * 4.0 + 2.0
                    three = jnp.floor(code * 0.5) * 2.0 + 1.0
                    cand = jnp.where(held == 2.0, two, jnp.where(held == 3.0, three, code))
                    base_w = ((code - 8.0) * scale).astype(BF16).astype(F32)
                    cand_w = ((cand - 8.0) * scale).astype(BF16).astype(F32)
                    base_acc[start : start + padded, cols] = base_w
                    diff_acc[start : start + padded, cols] = cand_w - base_w
            base_acc[top + 2 * rows : top + LANES, :] = blank
            diff_acc[top + 2 * rows : top + LANES, :] = blank
        block = pl.ds(yd * 4 * LANES, 4 * LANES)
        base[block, :] = base_acc[block, :].astype(BF16)
        diff[block, :] = diff_acc[block, :].astype(BF16)
        copies.append(pltpu.make_async_copy(base.at[block, :], base_hbm.at[block, :], sems.at[2 * yd]))
        copies.append(pltpu.make_async_copy(diff.at[block, :], diff_hbm.at[block, :], sems.at[2 * yd + 1]))
        copies[-2].start()
        copies[-1].start()
    for copy in copies:
        copy.wait()


def matmul_kernel(tokens, base_hbm, diff_hbm, out, left, base_w, diff_w, sems):
    rows, wide = tokens.shape[1:]
    copies = [
        pltpu.make_async_copy(base_hbm, base_w, sems.at[0]),
        pltpu.make_async_copy(diff_hbm, diff_w, sems.at[1]),
    ]
    for copy in copies:
        copy.start()
    factor = 1.0 / math.sqrt(HB * 16)
    for xd in range(4):
        s = [tokens[xd * 4 + yd].astype(F32) for yd in range(4)]
        a, b, c, d = s[0] + s[1], s[0] - s[1], s[2] + s[3], s[2] - s[3]
        for j, mixed in enumerate((a + c, b + d, a - c, b - d)):
            left[xd * rows : (xd + 1) * rows, j * wide : (j + 1) * wide] = (mixed * factor).astype(BF16)
    copies[0].wait()
    base = jnp.dot(left[...], base_w[...], preferred_element_type=F32).astype(BF16)
    copies[1].wait()
    diff = jnp.dot(left[...], diff_w[...], preferred_element_type=F32).astype(BF16)
    for xd in range(4):
        out[xd, 0:rows, :] = base[xd * rows : (xd + 1) * rows, :]
        out[xd, rows : 2 * rows, :] = diff[xd * rows : (xd + 1) * rows, :]


def unpad_kernel(parts, out):
    toks = parts.shape[1]
    for k in range(4):
        out[k * toks : (k + 1) * toks, :] = parts[k].astype(F32)


def spread_kernel(got, value, sign, out):
    mixed = (got[...] + sign[0] * value[...]).astype(BF16)
    for k in range(out.shape[0]):
        out[k] = mixed


def near_kernel(parts, out):
    total = parts[0].astype(F32)
    for k in range(1, 4):
        total = total + parts[k].astype(F32)
    for zd in range(4):
        out[zd] = total[:, zd * LANES : (zd + 1) * LANES].astype(BF16)


def far_kernel(parts, out, total, turn, block):
    acc = parts[0].astype(F32)
    for k in range(1, 4):
        acc = acc + parts[k].astype(F32)
    total[...] = acc
    rows = parts.shape[1] // 2
    toks = rows // 4
    gap = total[rows:, :]
    turn[rows:, :] = jnp.zeros((LANES - rows, LANES), F32)
    turn[0:rows, :] = jnp.broadcast_to(jnp.sum(gap * gap, axis=1, keepdims=True), (rows, LANES))
    score = turn[...].T[0:1, :]
    high = score.astype(BF16).astype(F32)
    middle = (score - high).astype(BF16).astype(F32)
    block[toks : toks + 1, :] = high
    block[toks + 1 : toks + 2, :] = middle
    block[toks + 2 : toks + 3, :] = score - high - middle
    block[toks + 3 : toks + 4, :] = jnp.zeros((1, LANES), F32)
    for yd in range(4):
        block[0:toks, :] = total[yd * toks : (yd + 1) * toks, :]
        wire = block[...].astype(BF16)
        out[yd] = wire
        out[4 + yd] = wire


def join_kernel(parts, place, base, line, held):
    toks = parts.shape[1] - 4
    c, y = place[2], place[3]
    lane = lax.broadcasted_iota(jnp.int32, (LANES, LANES), 0)
    slot = lax.broadcasted_iota(jnp.int32, (LANES, LANES), 1)
    final = jnp.zeros((8, LANES), F32)
    for cs in range(2):
        total = jnp.zeros((8, LANES), F32)
        for ys in range(4):
            total = total + parts[4 * cs + ys, toks - 4 : toks + 4, :].astype(F32)
        row = total[4:5, :] + total[5:6, :] + total[6:7, :]
        pick = jnp.where((lane == y * toks + slot - cs * toks) & (slot >= cs * toks) & (slot < (cs + 1) * toks), 1.0, 0.0)
        final = final + jnp.dot(jnp.broadcast_to(row, (8, LANES)), pick, precision=lax.Precision.HIGHEST, preferred_element_type=F32)
        for i in range(2):
            held[cs * toks : (cs + 1) * toks, i * LANES : (i + 1) * LANES] = parts[4 * cs + 2 * c + i][0:toks, :].astype(F32)
    base[...] = held[...].astype(BF16)
    for k in range(line.shape[0]):
        line[k] = final[0:1, :]


def last_kernel(lines, score):
    row = lines[0]
    for k in range(1, lines.shape[0]):
        row = row + lines[k]
    score[...] = row[:, 0 : score.shape[1]] * (1.0 / SCORE_DIVISOR)


def trade(value, axis, bit, size=4):
    return lax.ppermute(value, axis, [(i, i ^ bit) for i in range(size)])


def local(activations, weight_codes, scale_index, scale_table, bit_widths):
  place = jnp.stack([lax.axis_index(a) for a in ("x", "zh", "c", "y")]).astype(jnp.int32)
  toks, feat = activations.shape
  store, width = weight_codes.shape
  part = width // 16
  padded = store + 4
  wire = call(
      pack_kernel, jax.ShapeDtypeStruct((16, padded, part), BF16),
      [pl.BlockSpec(memory_space=pl.ANY), VMEM, VMEM],
      [pltpu.VMEM((store, width), jnp.int32), pltpu.VMEM((128, 128), F32), pltpu.VMEM((128, 128), F32),
       pltpu.VMEM((padded, part), F32), pltpu.SemaphoreType.DMA((4,))],
      0, store * width * 6, 60,
  )(weight_codes, scale_index, bit_widths.reshape(store, 1, -1))
  home = lax.all_to_all(wire, ("x", "y"), 0, 0, tiled=True)
  other = trade(home, "c", 1, 2)

  value = call(
      block_kernel, jax.ShapeDtypeStruct((4, toks, 4 * LANES), BF16), [VMEM] * 2,
      [pltpu.VMEM((feat // HB, toks + 4, HB), F32)], 2 * toks * 4096 * HB, 1 << 18, 4,
  )(activations, jnp.asarray(SIGNS, BF16))
  value = lax.all_to_all(value, "zh", 0, 0, tiled=True)
  value = call(unpad_kernel, jax.ShapeDtypeStruct((4 * toks, 4 * LANES), F32), [VMEM], (), 0, 1 << 18, 4)(value)
  sign = jnp.where(lax.axis_index("zl") & 1, -1.0, 1.0).astype(F32)
  value = trade(value, "zl", 1) + sign * value
  got = trade(value, "zl", 2)
  sign = jnp.where(lax.axis_index("zl") & 2, -1.0, 1.0).astype(F32).reshape(1)
  value = call(
      spread_kernel, jax.ShapeDtypeStruct((16,) + value.shape, BF16), [VMEM, VMEM, SMEM], (), 0, 1 << 21, 8,
  )(got, value, sign)
  tokens = lax.all_to_all(value, ("x", "y"), 0, 0, tiled=True)

  base_w, diff_w = pl.pallas_call(
      lambda *refs: weight_kernel(store, *refs),
      out_shape=[jax.ShapeDtypeStruct((16 * LANES, part), BF16)] * 2,
      in_specs=[VMEM, VMEM, SMEM, SMEM], out_specs=[HBM, HBM],
      scratch_shapes=[pltpu.VMEM((128, 128), F32)] + [pltpu.VMEM((16 * LANES, part), F32)] * 2
      + [pltpu.VMEM((16 * LANES, part), BF16)] * 2 + [pltpu.SemaphoreType.DMA((8,))],
      name="weights", compiler_params=pltpu.CompilerParams(vmem_limit_bytes=int(62.05 * (1 << 20))),
      cost_estimate=pl.CostEstimate(flops=feat * part * 20, bytes_accessed=feat * part * 6, transcendentals=0),
  )(home, other, scale_table, place)
  sums = call(
      matmul_kernel, jax.ShapeDtypeStruct((4, 8 * toks, part), BF16),
      [VMEM, HBM, HBM],
      [pltpu.VMEM((16 * toks, 16 * LANES), BF16)] + [pltpu.VMEM((16 * LANES, part), BF16)] * 2
      + [pltpu.SemaphoreType.DMA((2,))],
      4 * 16 * toks * feat * part, feat * part * 4 + 16 * toks * feat * 2, 52,
  )(tokens, base_w, diff_w)
  near = lax.all_to_all(sums, "zl", 0, 0, tiled=True)
  wave = call(
      near_kernel, jax.ShapeDtypeStruct((4, 8 * toks, LANES), BF16), [VMEM], (),
      32 * toks * part, 64 * toks * part, 8,
  )(near)
  far = lax.all_to_all(wave, "zh", 0, 0, tiled=True)
  wire = call(
      far_kernel, jax.ShapeDtypeStruct((8, toks + 4, LANES), BF16), [VMEM],
      [pltpu.VMEM((8 * toks, LANES), F32), pltpu.VMEM((LANES, LANES), F32), pltpu.VMEM((toks + 4, LANES), F32)],
      32 * toks * part, 40 * toks * part, 4,
  )(far)
  wire = lax.all_to_all(wire, ("c", "y"), 0, 0, tiled=True)
  base, line = call(
      join_kernel,
      [jax.ShapeDtypeStruct((2 * toks, 2 * LANES), BF16), jax.ShapeDtypeStruct((16, 1, LANES), F32)],
      [VMEM, SMEM], [pltpu.VMEM((2 * toks, 2 * LANES), F32)], 1 << 20, 1 << 18, 4,
  )(wire, place)
  lines = lax.all_to_all(line, ("x", "zh"), 0, 0, tiled=True)
  scores = call(last_kernel, jax.ShapeDtypeStruct((1, 2 * toks), F32), [VMEM], (), 1 << 12, 1 << 14, 4)(lines)
  return base, scores


def solution(mesh):
    fine = Mesh(mesh.devices.reshape(SIZES), AXES)
    dp, tensor = ("x", "zh", "c"), ("zl", "y")
    return jax.shard_map(
        local, mesh=fine,
        in_specs=(P(dp, tensor), P(tensor + dp, None), P(tensor + dp, None), P(), P(None, tensor + dp, None)),
        out_specs=(P(tensor, dp), P(None, tensor)),
        check_vma=False,
    )
```

```python
import math

import jax
import jax.numpy as jnp
import numpy as np
from jax import lax
from jax.experimental import pallas as pl
from jax.experimental.pallas import tpu as pltpu
from jax.sharding import Mesh, PartitionSpec as P


HB = 128
LANES = 128
AXES = ("x", "zh", "c", "zl", "y")
SIZES = (4, 4, 2, 4, 4)
CHUNK = 104
SCORE_DIVISOR = 512.0
F32 = jnp.float32
BF16 = jnp.bfloat16
VMEM = pl.BlockSpec(memory_space=pltpu.VMEM)
SMEM = pl.BlockSpec(memory_space=pltpu.SMEM)
HBM = pl.BlockSpec(memory_space=pltpu.HBM)


def block_signs():
    at = np.arange(HB)
    both = at[:, None] & at[None, :]
    parity = np.zeros((HB, HB), np.int64)
    for bit in range(7):
        parity ^= both >> bit & 1
    return (1 - 2 * parity).astype(np.float32)


SIGNS = block_signs()


def call(kernel, out_shape, in_specs, scratch=(), flops=0, moved=0, limit=16):
    multi = isinstance(out_shape, (list, tuple))
    return pl.pallas_call(
        kernel,
        out_shape=out_shape,
        in_specs=in_specs,
        out_specs=[VMEM] * len(out_shape) if multi else VMEM,
        scratch_shapes=list(scratch),
        compiler_params=pltpu.CompilerParams(vmem_limit_bytes=int(limit * (1 << 20))),
        cost_estimate=pl.CostEstimate(flops=flops, bytes_accessed=moved, transcendentals=0),
    )


def block_kernel(act, signs, out, work):
    toks = act.shape[0]
    blocks = act.shape[1] // HB
    for n in range(blocks):
        work[n, 0:toks, :] = jnp.dot(act[:, n * HB : (n + 1) * HB], signs[...], preferred_element_type=F32)
    lane = lax.broadcasted_iota(jnp.int32, work.shape[1:], 1)
    for m in range(16):
        xd, zd = divmod(m, 4)
        n, offset = divmod(CHUNK * m, HB)
        piece = work[n]
        if offset:
            piece = pltpu.roll(piece, HB - offset, 1)
            if offset + CHUNK > HB:
                piece = jnp.where(lane < HB - offset, piece, pltpu.roll(work[n + 1], HB - offset, 1))
        piece = jnp.where(lane < CHUNK, piece, 0.0)
        out[zd, :, xd * LANES : (xd + 1) * LANES] = piece[0:toks, :].astype(BF16)


def pack_kernel(codes_hbm, index, bits, out, codes, meta, turned, block, sems):
    rows, width = codes.shape
    quarter = width // 4
    groups = index.shape[1]
    copies = []
    for xd in range(4):
        cols = pl.ds(xd * quarter, quarter)
        copies.append(pltpu.make_async_copy(codes_hbm.at[:, cols], codes.at[:, cols], sems.at[xd]))
        copies[-1].start()
    meta[...] = jnp.zeros_like(meta)
    meta[0:rows, 0:groups] = index[...].astype(F32)
    meta[0:rows, groups : 2 * groups] = bits[:, 0, :].astype(F32)
    turned[...] = meta[...].T
    block[...] = jnp.zeros_like(block)
    for xd in range(4):
        copies[xd].wait()
        for yd in range(4):
            for k in range(4):
                g = 16 * xd + 4 * k + yd
                block[0:rows, k * LANES : (k + 1) * LANES] = codes[:, g * LANES : (g + 1) * LANES].astype(F32)
                block[rows + k : rows + k + 1, 0:LANES] = turned[g : g + 1, :]
                block[rows + k : rows + k + 1, LANES : 2 * LANES] = turned[groups + g : groups + g + 1, :]
            out[xd * 4 + yd] = block[...].astype(BF16)


def weight_kernel(rows, own, other, table, place, base_hbm, diff_hbm, meta, base_acc, diff_acc, base, diff, sems):
    padded = own.shape[1]
    first = place[2] == 0
    turned = []
    for core in range(2):
        mine, theirs = (own, other) if core == 0 else (other, own)
        for p in range(16):
            tail = jnp.where(first, mine[p, padded - 8 : padded, :].astype(F32), theirs[p, padded - 8 : padded, :].astype(F32))
            meta[p * 4 : p * 4 + 4, :] = tail[4:, 0:LANES]
            meta[64 + p * 4 : 68 + p * 4, :] = tail[4:, LANES : 2 * LANES]
        index = meta[0:64, :]
        scale = jnp.zeros_like(index)
        for entry in range(table.shape[0]):
            scale = jnp.where(index == float(entry), table[entry], scale)
        meta[0:64, :] = scale
        turned.append(meta[...].T)
    blank = jnp.zeros((LANES - 2 * rows, own.shape[2]), F32)
    copies = []
    for yd in range(4):
        for xd in range(4):
            p = xd * 4 + yd
            top = (yd * 4 + xd) * LANES
            for core in range(2):
                mine, theirs = (own, other) if core == 0 else (other, own)
                start = top + core * rows
                for k in range(4):
                    cols = slice(k * LANES, (k + 1) * LANES)
                    code = jnp.where(first, mine[p, :, cols], theirs[p, :, cols]).astype(F32)
                    at = p * 4 + k
                    scale = turned[core][0:padded, at : at + 1]
                    held = turned[core][0:padded, 64 + at : 65 + at]
                    two = jnp.floor(code * 0.25) * 4.0 + 2.0
                    three = jnp.floor(code * 0.5) * 2.0 + 1.0
                    cand = jnp.where(held == 2.0, two, jnp.where(held == 3.0, three, code))
                    base_w = ((code - 8.0) * scale).astype(BF16).astype(F32)
                    cand_w = ((cand - 8.0) * scale).astype(BF16).astype(F32)
                    base_acc[start : start + padded, cols] = base_w
                    diff_acc[start : start + padded, cols] = cand_w - base_w
            base_acc[top + 2 * rows : top + LANES, :] = blank
            diff_acc[top + 2 * rows : top + LANES, :] = blank
        block = pl.ds(yd * 4 * LANES, 4 * LANES)
        base[block, :] = base_acc[block, :].astype(BF16)
        diff[block, :] = diff_acc[block, :].astype(BF16)
        copies.append(pltpu.make_async_copy(base.at[block, :], base_hbm.at[block, :], sems.at[2 * yd]))
        copies.append(pltpu.make_async_copy(diff.at[block, :], diff_hbm.at[block, :], sems.at[2 * yd + 1]))
        copies[-2].start()
        copies[-1].start()
    for copy in copies:
        copy.wait()


def matmul_kernel(tokens, base_hbm, diff_hbm, out, left, base_w, diff_w, sems):
    rows, wide = tokens.shape[1:]
    copies = [
        pltpu.make_async_copy(base_hbm, base_w, sems.at[0]),
        pltpu.make_async_copy(diff_hbm, diff_w, sems.at[1]),
    ]
    for copy in copies:
        copy.start()
    factor = 1.0 / math.sqrt(HB * 16)
    for xd in range(4):
        s = [tokens[xd * 4 + yd].astype(F32) for yd in range(4)]
        a, b, c, d = s[0] + s[1], s[0] - s[1], s[2] + s[3], s[2] - s[3]
        for j, mixed in enumerate((a + c, b + d, a - c, b - d)):
            left[xd * rows : (xd + 1) * rows, j * wide : (j + 1) * wide] = (mixed * factor).astype(BF16)
    copies[0].wait()
    base = jnp.dot(left[...], base_w[...], preferred_element_type=F32).astype(BF16)
    copies[1].wait()
    diff = jnp.dot(left[...], diff_w[...], preferred_element_type=F32).astype(BF16)
    for xd in range(4):
        out[xd, 0:rows, :] = base[xd * rows : (xd + 1) * rows, :]
        out[xd, rows : 2 * rows, :] = diff[xd * rows : (xd + 1) * rows, :]


def unpad_kernel(parts, out, work):
    toks = parts.shape[1]
    for k in range(4):
        work[k * toks : (k + 1) * toks, :] = parts[k].astype(F32)
    out[...] = work[...].astype(BF16)


def spread_kernel(own, g1, g2, g3, signs, out):
    mixed = signs[0] * own[...].astype(F32)
    for k, got in enumerate((g1, g2, g3)):
        mixed = mixed + signs[k + 1] * got[...].astype(F32)
    mixed = mixed.astype(BF16)
    for k in range(out.shape[0]):
        out[k] = mixed


def near_kernel(parts, out, total, both):
    acc = parts[0].astype(F32)
    for k in range(1, 4):
        acc = acc + parts[k].astype(F32)
    total[...] = acc
    rows = parts.shape[1] // 2
    toks = rows // 4
    for zd in range(4):
        cols = slice(zd * LANES, (zd + 1) * LANES)
        for yd in range(4):
            both[0:toks, :] = total[yd * toks : (yd + 1) * toks, cols]
            both[toks : 2 * toks, :] = total[rows + yd * toks : rows + (yd + 1) * toks, cols]
            out[zd * 4 + yd] = both[...].astype(BF16)


def far_kernel(parts, place, line, keep, send, both, turn, halves):
    toks = parts.shape[1] // 2
    score = jnp.zeros((toks, LANES), F32)
    for ys in range(4):
        acc = parts[ys].astype(F32)
        for zs in range(1, 4):
            acc = acc + parts[zs * 4 + ys].astype(F32)
        both[...] = acc
        gap = both[toks : 2 * toks, :]
        score = score + gap * gap
        halves[ys // 2, :, (ys % 2) * LANES : (ys % 2 + 1) * LANES] = both[0:toks, :]
    turn[...] = jnp.zeros_like(turn)
    turn[0:toks, :] = jnp.broadcast_to(jnp.sum(score, axis=1, keepdims=True), (toks, LANES))
    row = turn[...].T[0:1, :]
    for k in range(line.shape[0]):
        line[k] = row
    keep[...] = halves[place[2]].astype(BF16)
    send[...] = halves[1 - place[2]].astype(BF16)


def last_kernel(lines, keep, got, place, base, score, held):
    toks = keep.shape[0]
    first = place[2] == 0
    mine, theirs = keep[...].astype(F32), got[...].astype(F32)
    held[0:toks, :] = jnp.where(first, mine, theirs)
    held[toks : 2 * toks, :] = jnp.where(first, theirs, mine)
    base[...] = held[...].astype(BF16)
    rows = []
    for cs in range(2):
        row = lines[cs]
        for k in range(1, lines.shape[0] // 2):
            row = row + lines[2 * k + cs]
        rows.append(row)
    lane = lax.broadcasted_iota(jnp.int32, rows[0].shape, 1)
    both = jnp.where(lane < toks, rows[0], pltpu.roll(rows[1], toks, 1))
    score[...] = both[:, 0 : 2 * toks] * (1.0 / SCORE_DIVISOR)


def trade(value, axis, bit, size=4):
    return lax.ppermute(value, axis, [(i, i ^ bit) for i in range(size)])


def local(activations, weight_codes, scale_index, scale_table, bit_widths):
  place = jnp.stack([lax.axis_index(a) for a in ("x", "zh", "c", "y")]).astype(jnp.int32)
  toks, feat = activations.shape
  store, width = weight_codes.shape
  part = width // 16
  padded = store + 4
  wire = call(
      pack_kernel, jax.ShapeDtypeStruct((16, padded, part), BF16),
      [pl.BlockSpec(memory_space=pl.ANY), VMEM, VMEM],
      [pltpu.VMEM((store, width), jnp.int32), pltpu.VMEM((128, 128), F32), pltpu.VMEM((128, 128), F32),
       pltpu.VMEM((padded, part), F32), pltpu.SemaphoreType.DMA((4,))],
      0, store * width * 6, 60,
  )(weight_codes, scale_index, bit_widths.reshape(store, 1, -1))
  home = lax.all_to_all(wire, ("x", "y"), 0, 0, tiled=True)
  other = trade(home, "c", 1, 2)

  value = call(
      block_kernel, jax.ShapeDtypeStruct((4, toks, 4 * LANES), BF16), [VMEM] * 2,
      [pltpu.VMEM((feat // HB, toks + 4, HB), F32)], 2 * toks * 4096 * HB, 1 << 18, 61,
  )(activations, jnp.asarray(SIGNS, BF16))
  value = lax.all_to_all(value, "zh", 0, 0, tiled=True)
  value = call(
      unpad_kernel, jax.ShapeDtypeStruct((4 * toks, 4 * LANES), BF16), [VMEM],
      [pltpu.VMEM((4 * toks, 4 * LANES), F32)], 0, 1 << 18, 4,
  )(value)
  got = []
  for k in (1, 2, 3):
      got.append(trade(value, "zl", k))
  zl = lax.axis_index("zl")
  common = [zl & (zl ^ k) for k in range(4)]
  signs = jnp.stack([1 - 2 * ((v ^ (v >> 1)) & 1) for v in common]).astype(F32)
  value = call(
      spread_kernel, jax.ShapeDtypeStruct((16,) + value.shape, BF16), [VMEM] * 4 + [SMEM], (), 0, 1 << 21, 8,
  )(value, *got, signs)
  tokens = lax.all_to_all(value, ("x", "y"), 0, 0, tiled=True)

  base_w, diff_w = pl.pallas_call(
      lambda *refs: weight_kernel(store, *refs),
      out_shape=[jax.ShapeDtypeStruct((16 * LANES, part), BF16)] * 2,
      in_specs=[VMEM, VMEM, SMEM, SMEM], out_specs=[HBM, HBM],
      scratch_shapes=[pltpu.VMEM((128, 128), F32)] + [pltpu.VMEM((16 * LANES, part), F32)] * 2
      + [pltpu.VMEM((16 * LANES, part), BF16)] * 2 + [pltpu.SemaphoreType.DMA((8,))],
      name="weights", compiler_params=pltpu.CompilerParams(vmem_limit_bytes=int(62.05 * (1 << 20))),
      cost_estimate=pl.CostEstimate(flops=feat * part * 20, bytes_accessed=feat * part * 6, transcendentals=0),
  )(home, other, scale_table, place)
  sums = call(
      matmul_kernel, jax.ShapeDtypeStruct((4, 8 * toks, part), BF16),
      [VMEM, HBM, HBM],
      [pltpu.VMEM((16 * toks, 16 * LANES), BF16)] + [pltpu.VMEM((16 * LANES, part), BF16)] * 2
      + [pltpu.SemaphoreType.DMA((2,))],
      4 * 16 * toks * feat * part, feat * part * 4 + 16 * toks * feat * 2, 52,
  )(tokens, base_w, diff_w)
  near = lax.all_to_all(sums, "zl", 0, 0, tiled=True)
  wave = call(
      near_kernel, jax.ShapeDtypeStruct((16, 2 * toks, LANES), BF16), [VMEM],
      [pltpu.VMEM((8 * toks, part), F32), pltpu.VMEM((2 * toks, LANES), F32)],
      32 * toks * part, 64 * toks * part, 8,
  )(near)
  far = lax.all_to_all(wave, ("zh", "y"), 0, 0, tiled=True)
  line, keep, send = call(
      far_kernel,
      [jax.ShapeDtypeStruct((32, 1, LANES), F32)] + [jax.ShapeDtypeStruct((toks, 2 * LANES), BF16)] * 2,
      [VMEM, SMEM],
      [pltpu.VMEM((2 * toks, LANES), F32), pltpu.VMEM((LANES, LANES), F32), pltpu.VMEM((2, toks, 2 * LANES), F32)],
      32 * toks * part, 40 * toks * part, 4,
  )(far, place)
  lines = lax.all_to_all(line, ("x", "zh", "c"), 0, 0, tiled=True)
  got = trade(send, "c", 1, 2)
  base, scores = call(
      last_kernel,
      [jax.ShapeDtypeStruct((2 * toks, 2 * LANES), BF16), jax.ShapeDtypeStruct((1, 2 * toks), F32)],
      [VMEM] * 3 + [SMEM], [pltpu.VMEM((2 * toks, 2 * LANES), F32)], 1 << 16, 1 << 16, 4,
  )(lines, keep, got, place)
  return base, scores


def solution(mesh):
    fine = Mesh(mesh.devices.reshape(SIZES), AXES)
    dp, tensor = ("x", "zh", "c"), ("zl", "y")
    return jax.shard_map(
        local, mesh=fine,
        in_specs=(P(dp, tensor), P(tensor + dp, None), P(tensor + dp, None), P(), P(None, tensor + dp, None)),
        out_specs=(P(tensor, dp), P(None, tensor)),
        check_vma=False,
    )
```

```python
import math

import jax
import jax.numpy as jnp
import numpy as np
from jax import lax
from jax.experimental import pallas as pl
from jax.experimental.pallas import tpu as pltpu
from jax.sharding import Mesh, PartitionSpec as P


HB = 128
LANES = 128
AXES = ("x", "zh", "c", "zl", "y")
SIZES = (4, 4, 2, 4, 4)
CHUNK = 104
SCORE_DIVISOR = 512.0
F32 = jnp.float32
BF16 = jnp.bfloat16
VMEM = pl.BlockSpec(memory_space=pltpu.VMEM)
SMEM = pl.BlockSpec(memory_space=pltpu.SMEM)
HBM = pl.BlockSpec(memory_space=pltpu.HBM)


def block_signs():
    at = np.arange(HB)
    both = at[:, None] & at[None, :]
    parity = np.zeros((HB, HB), np.int64)
    for bit in range(7):
        parity ^= both >> bit & 1
    return (1 - 2 * parity).astype(np.float32)


SIGNS = block_signs()


def call(kernel, out_shape, in_specs, scratch=(), flops=0, moved=0, limit=16):
    multi = isinstance(out_shape, (list, tuple))
    return pl.pallas_call(
        kernel,
        out_shape=out_shape,
        in_specs=in_specs,
        out_specs=[VMEM] * len(out_shape) if multi else VMEM,
        scratch_shapes=list(scratch),
        compiler_params=pltpu.CompilerParams(vmem_limit_bytes=int(limit * (1 << 20))),
        cost_estimate=pl.CostEstimate(flops=flops, bytes_accessed=moved, transcendentals=0),
    )


def block_kernel(act, signs, out, work):
    toks = act.shape[0]
    blocks = act.shape[1] // HB
    for n in range(blocks):
        work[n, 0:toks, :] = jnp.dot(act[:, n * HB : (n + 1) * HB], signs[...], preferred_element_type=F32)
    lane = lax.broadcasted_iota(jnp.int32, work.shape[1:], 1)
    for m in range(16):
        xd, zd = divmod(m, 4)
        n, offset = divmod(CHUNK * m, HB)
        piece = work[n]
        if offset:
            piece = pltpu.roll(piece, HB - offset, 1)
            if offset + CHUNK > HB:
                piece = jnp.where(lane < HB - offset, piece, pltpu.roll(work[n + 1], HB - offset, 1))
        piece = jnp.where(lane < CHUNK, piece, 0.0)
        out[zd, :, xd * LANES : (xd + 1) * LANES] = piece[0:toks, :].astype(BF16)


def pack_kernel(codes_hbm, index, bits, out, codes, meta, turned, block, sems):
    rows, width = codes.shape
    quarter = width // 4
    groups = index.shape[1]
    copies = []
    for xd in range(4):
        cols = pl.ds(xd * quarter, quarter)
        copies.append(pltpu.make_async_copy(codes_hbm.at[:, cols], codes.at[:, cols], sems.at[xd]))
        copies[-1].start()
    meta[...] = jnp.zeros_like(meta)
    meta[0:rows, 0:groups] = index[...].astype(F32)
    meta[0:rows, groups : 2 * groups] = bits[:, 0, :].astype(F32)
    turned[...] = meta[...].T
    block[...] = jnp.zeros_like(block)
    for xd in range(4):
        copies[xd].wait()
        for yd in range(4):
            for k in range(4):
                g = 16 * xd + 4 * k + yd
                block[0:rows, k * LANES : (k + 1) * LANES] = codes[:, g * LANES : (g + 1) * LANES].astype(F32)
                block[rows + k : rows + k + 1, 0:LANES] = turned[g : g + 1, :]
                block[rows + k : rows + k + 1, LANES : 2 * LANES] = turned[groups + g : groups + g + 1, :]
            out[xd * 4 + yd] = block[...].astype(BF16)


def weight_kernel(rows, own, other, table, place, base_hbm, diff_hbm, meta, base_acc, diff_acc, base, diff, sems):
    padded = own.shape[1]
    first = place[2] == 0
    turned = []
    for core in range(2):
        mine, theirs = (own, other) if core == 0 else (other, own)
        for p in range(16):
            tail = jnp.where(first, mine[p, padded - 8 : padded, :].astype(F32), theirs[p, padded - 8 : padded, :].astype(F32))
            meta[p * 4 : p * 4 + 4, :] = tail[4:, 0:LANES]
            meta[64 + p * 4 : 68 + p * 4, :] = tail[4:, LANES : 2 * LANES]
        index = meta[0:64, :]
        scale = jnp.zeros_like(index)
        for entry in range(table.shape[0]):
            scale = jnp.where(index == float(entry), table[entry], scale)
        meta[0:64, :] = scale
        turned.append(meta[...].T)
    blank = jnp.zeros((LANES - 2 * rows, own.shape[2]), F32)
    copies = []
    for yd in range(4):
        for xd in range(4):
            p = xd * 4 + yd
            top = (yd * 4 + xd) * LANES
            for core in range(2):
                mine, theirs = (own, other) if core == 0 else (other, own)
                start = top + core * rows
                for k in range(4):
                    cols = slice(k * LANES, (k + 1) * LANES)
                    code = jnp.where(first, mine[p, :, cols], theirs[p, :, cols]).astype(F32)
                    at = p * 4 + k
                    scale = turned[core][0:padded, at : at + 1]
                    held = turned[core][0:padded, 64 + at : 65 + at]
                    two = jnp.floor(code * 0.25) * 4.0 + 2.0
                    three = jnp.floor(code * 0.5) * 2.0 + 1.0
                    cand = jnp.where(held == 2.0, two, jnp.where(held == 3.0, three, code))
                    base_w = ((code - 8.0) * scale).astype(BF16).astype(F32)
                    cand_w = ((cand - 8.0) * scale).astype(BF16).astype(F32)
                    base_acc[start : start + padded, cols] = base_w
                    diff_acc[start : start + padded, cols] = cand_w - base_w
            base_acc[top + 2 * rows : top + LANES, :] = blank
            diff_acc[top + 2 * rows : top + LANES, :] = blank
        block = pl.ds(yd * 4 * LANES, 4 * LANES)
        base[block, :] = base_acc[block, :].astype(BF16)
        diff[block, :] = diff_acc[block, :].astype(BF16)
        copies.append(pltpu.make_async_copy(base.at[block, :], base_hbm.at[block, :], sems.at[2 * yd]))
        copies.append(pltpu.make_async_copy(diff.at[block, :], diff_hbm.at[block, :], sems.at[2 * yd + 1]))
        copies[-2].start()
        copies[-1].start()
    for copy in copies:
        copy.wait()


def matmul_kernel(tokens, base_hbm, diff_hbm, out, left, base_w, diff_w, base_acc, diff_acc, both, sems):
    rows, wide = tokens.shape[1:]
    toks = rows // 4
    copies = []
    for j in range(4):
        block = pl.ds(j * wide, wide)
        for source, target in ((base_hbm, base_w), (diff_hbm, diff_w)):
            copies.append(pltpu.make_async_copy(source.at[block, :], target.at[block, :], sems.at[len(copies)]))
            copies[-1].start()
    factor = 1.0 / math.sqrt(HB * 16)
    for xd in range(4):
        s = [tokens[xd * 4 + yd].astype(F32) for yd in range(4)]
        a, b, c, d = s[0] + s[1], s[0] - s[1], s[2] + s[3], s[2] - s[3]
        for j, mixed in enumerate((a + c, b + d, a - c, b - d)):
            left[xd * rows : (xd + 1) * rows, j * wide : (j + 1) * wide] = (mixed * factor).astype(BF16)
    for j in range(4):
        block = slice(j * wide, (j + 1) * wide)
        for k, (weight, total) in enumerate(((base_w, base_acc), (diff_w, diff_acc))):
            copies[2 * j + k].wait()
            part = jnp.dot(left[:, block], weight[block, :], preferred_element_type=F32)
            total[...] = part if j == 0 else total[...] + part
    for xd in range(4):
        for yd in range(4):
            start = xd * rows + yd * toks
            both[0:toks, :] = base_acc[start : start + toks, :]
            both[toks : 2 * toks, :] = diff_acc[start : start + toks, :]
            out[xd * 4 + yd] = both[...].astype(BF16)


def unpad_kernel(parts, out, work):
    toks = parts.shape[1]
    for k in range(4):
        work[k * toks : (k + 1) * toks, :] = parts[k].astype(F32)
    out[...] = work[...].astype(BF16)


def spread_kernel(own, g1, g2, g3, signs, out):
    mixed = signs[0] * own[...].astype(F32)
    for k, got in enumerate((g1, g2, g3)):
        mixed = mixed + signs[k + 1] * got[...].astype(F32)
    mixed = mixed.astype(BF16)
    for k in range(out.shape[0]):
        out[k] = mixed


def near_kernel(parts, out):
    rows = parts.shape[1]
    for ys in range(4):
        acc = parts[ys].astype(F32)
        for zs in range(1, 4):
            acc = acc + parts[zs * 4 + ys].astype(F32)
        for zd in range(4):
            out[zd, ys * rows : (ys + 1) * rows, :] = acc[:, zd * LANES : (zd + 1) * LANES].astype(BF16)


def far_kernel(parts, place, line, keep, send, both, turn, halves):
    rows = parts.shape[1] // 4
    toks = rows // 2
    score = jnp.zeros((toks, LANES), F32)
    for ys in range(4):
        block = slice(ys * rows, (ys + 1) * rows)
        acc = parts[0, block, :].astype(F32)
        for zs in range(1, 4):
            acc = acc + parts[zs, block, :].astype(F32)
        both[...] = acc
        gap = both[toks : 2 * toks, :]
        score = score + gap * gap
        halves[ys // 2, :, (ys % 2) * LANES : (ys % 2 + 1) * LANES] = both[0:toks, :]
    turn[...] = jnp.zeros_like(turn)
    turn[0:toks, :] = jnp.broadcast_to(jnp.sum(score, axis=1, keepdims=True), (toks, LANES))
    row = turn[...].T[0:1, :]
    for k in range(line.shape[0]):
        line[k] = row
    keep[...] = halves[place[2]].astype(BF16)
    send[...] = halves[1 - place[2]].astype(BF16)


def base_kernel(keep, got, place, base, held):
    toks = keep.shape[0]
    first = place[2] == 0
    mine, theirs = keep[...].astype(F32), got[...].astype(F32)
    held[0:toks, :] = jnp.where(first, mine, theirs)
    held[toks : 2 * toks, :] = jnp.where(first, theirs, mine)
    base[...] = held[...].astype(BF16)


def last_kernel(lines, score):
    toks = score.shape[1] // 2
    rows = []
    for cs in range(2):
        row = lines[cs]
        for k in range(1, lines.shape[0] // 2):
            row = row + lines[2 * k + cs]
        rows.append(row)
    lane = lax.broadcasted_iota(jnp.int32, rows[0].shape, 1)
    both = jnp.where(lane < toks, rows[0], pltpu.roll(rows[1], toks, 1))
    score[...] = both[:, 0 : 2 * toks] * (1.0 / SCORE_DIVISOR)


def trade(value, axis, bit, size=4):
    return lax.ppermute(value, axis, [(i, i ^ bit) for i in range(size)])


def local(activations, weight_codes, scale_index, scale_table, bit_widths):
  place = jnp.stack([lax.axis_index(a) for a in ("x", "zh", "c", "y")]).astype(jnp.int32)
  toks, feat = activations.shape
  store, width = weight_codes.shape
  part = width // 16
  padded = store + 4
  wire = call(
      pack_kernel, jax.ShapeDtypeStruct((16, padded, part), BF16),
      [pl.BlockSpec(memory_space=pl.ANY), VMEM, VMEM],
      [pltpu.VMEM((store, width), jnp.int32), pltpu.VMEM((128, 128), F32), pltpu.VMEM((128, 128), F32),
       pltpu.VMEM((padded, part), F32), pltpu.SemaphoreType.DMA((4,))],
      0, store * width * 6, 60,
  )(weight_codes, scale_index, bit_widths.reshape(store, 1, -1))
  home = lax.all_to_all(wire, ("x", "y"), 0, 0, tiled=True)
  other = trade(home, "c", 1, 2)

  value = call(
      block_kernel, jax.ShapeDtypeStruct((4, toks, 4 * LANES), BF16), [VMEM] * 2,
      [pltpu.VMEM((feat // HB, toks + 4, HB), F32)], 2 * toks * 4096 * HB, 1 << 18, 61,
  )(activations, jnp.asarray(SIGNS, BF16))
  value = lax.all_to_all(value, "zh", 0, 0, tiled=True)
  value = call(
      unpad_kernel, jax.ShapeDtypeStruct((4 * toks, 4 * LANES), BF16), [VMEM],
      [pltpu.VMEM((4 * toks, 4 * LANES), F32)], 0, 1 << 18, 4,
  )(value)
  got = []
  for k in (1, 2, 3):
      got.append(trade(value, "zl", k))
  zl = lax.axis_index("zl")
  common = [zl & (zl ^ k) for k in range(4)]
  signs = jnp.stack([1 - 2 * ((v ^ (v >> 1)) & 1) for v in common]).astype(F32)
  value = call(
      spread_kernel, jax.ShapeDtypeStruct((16,) + value.shape, BF16), [VMEM] * 4 + [SMEM], (), 0, 1 << 21, 8,
  )(value, *got, signs)
  tokens = lax.all_to_all(value, ("x", "y"), 0, 0, tiled=True)

  base_w, diff_w = pl.pallas_call(
      lambda *refs: weight_kernel(store, *refs),
      out_shape=[jax.ShapeDtypeStruct((16 * LANES, part), BF16)] * 2,
      in_specs=[VMEM, VMEM, SMEM, SMEM], out_specs=[HBM, HBM],
      scratch_shapes=[pltpu.VMEM((128, 128), F32)] + [pltpu.VMEM((16 * LANES, part), F32)] * 2
      + [pltpu.VMEM((16 * LANES, part), BF16)] * 2 + [pltpu.SemaphoreType.DMA((8,))],
      name="weights", compiler_params=pltpu.CompilerParams(vmem_limit_bytes=int(62.05 * (1 << 20))),
      cost_estimate=pl.CostEstimate(flops=feat * part * 20, bytes_accessed=feat * part * 6, transcendentals=0),
  )(home, other, scale_table, place)
  sums = call(
      matmul_kernel, jax.ShapeDtypeStruct((16, 2 * toks, part), BF16),
      [VMEM, HBM, HBM],
      [pltpu.VMEM((16 * toks, 16 * LANES), BF16)] + [pltpu.VMEM((16 * LANES, part), BF16)] * 2
      + [pltpu.VMEM((16 * toks, part), F32)] * 2 + [pltpu.VMEM((2 * toks, part), F32), pltpu.SemaphoreType.DMA((8,))],
      4 * 16 * toks * feat * part, feat * part * 4 + 16 * toks * feat * 2, 52,
  )(tokens, base_w, diff_w)
  near = lax.all_to_all(sums, ("zl", "y"), 0, 0, tiled=True)
  wave = call(
      near_kernel, jax.ShapeDtypeStruct((4, 8 * toks, LANES), BF16), [VMEM], (),
      32 * toks * part, 64 * toks * part, 8,
  )(near)
  far = lax.all_to_all(wave, "zh", 0, 0, tiled=True)
  line, keep, send = call(
      far_kernel,
      [jax.ShapeDtypeStruct((32, 1, LANES), F32)] + [jax.ShapeDtypeStruct((toks, 2 * LANES), BF16)] * 2,
      [VMEM, SMEM],
      [pltpu.VMEM((2 * toks, LANES), F32), pltpu.VMEM((LANES, LANES), F32), pltpu.VMEM((2, toks, 2 * LANES), F32)],
      32 * toks * part, 40 * toks * part, 4,
  )(far, place)
  lines = lax.all_to_all(line, ("x", "zh", "c"), 0, 0, tiled=True)
  got = trade(send, "c", 1, 2)
  base = call(
      base_kernel, jax.ShapeDtypeStruct((2 * toks, 2 * LANES), BF16), [VMEM, VMEM, SMEM],
      [pltpu.VMEM((2 * toks, 2 * LANES), F32)], 1 << 12, 1 << 16, 4,
  )(keep, got, place)
  scores = call(last_kernel, jax.ShapeDtypeStruct((1, 2 * toks), F32), [VMEM], (), 1 << 12, 1 << 14, 4)(lines)
  return base, scores


def solution(mesh):
    fine = Mesh(mesh.devices.reshape(SIZES), AXES)
    dp, tensor = ("x", "zh", "c"), ("zl", "y")
    return jax.shard_map(
        local, mesh=fine,
        in_specs=(P(dp, tensor), P(tensor + dp, None), P(tensor + dp, None), P(), P(None, tensor + dp, None)),
        out_specs=(P(tensor, dp), P(None, tensor)),
        check_vma=False,
    )
```

```python
import math

import jax
import jax.numpy as jnp
import numpy as np
from jax import lax
from jax.experimental import pallas as pl
from jax.experimental.pallas import tpu as pltpu
from jax.sharding import Mesh, PartitionSpec as P


HB = 128
LANES = 128
AXES = ("x", "zh", "c", "zl", "y")
SIZES = (4, 4, 2, 4, 4)
CHUNK = 104
SCORE_DIVISOR = 512.0
F32 = jnp.float32
BF16 = jnp.bfloat16
VMEM = pl.BlockSpec(memory_space=pltpu.VMEM)
SMEM = pl.BlockSpec(memory_space=pltpu.SMEM)
HBM = pl.BlockSpec(memory_space=pltpu.HBM)


def block_signs():
    at = np.arange(HB)
    both = at[:, None] & at[None, :]
    parity = np.zeros((HB, HB), np.int64)
    for bit in range(7):
        parity ^= both >> bit & 1
    return (1 - 2 * parity).astype(np.float32)


SIGNS = block_signs()


def call(kernel, out_shape, in_specs, scratch=(), flops=0, moved=0, limit=16):
    multi = isinstance(out_shape, (list, tuple))
    return pl.pallas_call(
        kernel,
        out_shape=out_shape,
        in_specs=in_specs,
        out_specs=[VMEM] * len(out_shape) if multi else VMEM,
        scratch_shapes=list(scratch),
        compiler_params=pltpu.CompilerParams(vmem_limit_bytes=int(limit * (1 << 20))),
        cost_estimate=pl.CostEstimate(flops=flops, bytes_accessed=moved, transcendentals=0),
    )


def block_kernel(act, signs, out, work):
    toks = act.shape[0]
    blocks = act.shape[1] // HB
    for n in range(blocks):
        work[n, 0:toks, :] = jnp.dot(act[:, n * HB : (n + 1) * HB], signs[...], preferred_element_type=F32)
    lane = lax.broadcasted_iota(jnp.int32, work.shape[1:], 1)
    for m in range(16):
        xd, zd = divmod(m, 4)
        n, offset = divmod(CHUNK * m, HB)
        piece = work[n]
        if offset:
            piece = pltpu.roll(piece, HB - offset, 1)
            if offset + CHUNK > HB:
                piece = jnp.where(lane < HB - offset, piece, pltpu.roll(work[n + 1], HB - offset, 1))
        piece = jnp.where(lane < CHUNK, piece, 0.0)
        out[zd, :, xd * LANES : (xd + 1) * LANES] = piece[0:toks, :].astype(BF16)


def pack_kernel(codes_hbm, index, bits, out, codes, meta, turned, block, sems):
    rows, width = codes.shape
    quarter = width // 4
    groups = index.shape[1]
    copies = []
    for xd in range(4):
        cols = pl.ds(xd * quarter, quarter)
        copies.append(pltpu.make_async_copy(codes_hbm.at[:, cols], codes.at[:, cols], sems.at[xd]))
        copies[-1].start()
    meta[...] = jnp.zeros_like(meta)
    meta[0:rows, 0:groups] = index[...].astype(F32)
    meta[0:rows, groups : 2 * groups] = bits[:, 0, :].astype(F32)
    turned[...] = meta[...].T
    block[...] = jnp.zeros_like(block)
    for xd in range(4):
        copies[xd].wait()
        for yd in range(4):
            for k in range(4):
                g = 16 * xd + 4 * k + yd
                block[0:rows, k * LANES : (k + 1) * LANES] = codes[:, g * LANES : (g + 1) * LANES].astype(F32)
                block[rows + k : rows + k + 1, 0:LANES] = turned[g : g + 1, :]
                block[rows + k : rows + k + 1, LANES : 2 * LANES] = turned[groups + g : groups + g + 1, :]
            out[xd * 4 + yd] = block[...].astype(BF16)


def weight_kernel(rows, own, other, table, place, base_hbm, diff_hbm, meta, base_acc, diff_acc, base, diff, sems):
    padded = own.shape[1]
    first = place[2] == 0
    turned = []
    for core in range(2):
        mine, theirs = (own, other) if core == 0 else (other, own)
        for p in range(16):
            tail = jnp.where(first, mine[p, padded - 8 : padded, :].astype(F32), theirs[p, padded - 8 : padded, :].astype(F32))
            meta[p * 4 : p * 4 + 4, :] = tail[4:, 0:LANES]
            meta[64 + p * 4 : 68 + p * 4, :] = tail[4:, LANES : 2 * LANES]
        index = meta[0:64, :]
        scale = jnp.zeros_like(index)
        for entry in range(table.shape[0]):
            scale = jnp.where(index == float(entry), table[entry], scale)
        meta[0:64, :] = scale
        turned.append(meta[...].T)
    blank = jnp.zeros((LANES - 2 * rows, own.shape[2]), F32)
    copies = []
    for yd in range(4):
        for xd in range(4):
            p = xd * 4 + yd
            top = (yd * 4 + xd) * LANES
            for core in range(2):
                mine, theirs = (own, other) if core == 0 else (other, own)
                start = top + core * rows
                for k in range(4):
                    cols = slice(k * LANES, (k + 1) * LANES)
                    code = jnp.where(first, mine[p, :, cols], theirs[p, :, cols]).astype(F32)
                    at = p * 4 + k
                    scale = turned[core][0:padded, at : at + 1]
                    held = turned[core][0:padded, 64 + at : 65 + at]
                    two = jnp.floor(code * 0.25) * 4.0 + 2.0
                    three = jnp.floor(code * 0.5) * 2.0 + 1.0
                    cand = jnp.where(held == 2.0, two, jnp.where(held == 3.0, three, code))
                    base_w = ((code - 8.0) * scale).astype(BF16).astype(F32)
                    cand_w = ((cand - 8.0) * scale).astype(BF16).astype(F32)
                    base_acc[start : start + padded, cols] = base_w
                    diff_acc[start : start + padded, cols] = cand_w - base_w
            base_acc[top + 2 * rows : top + LANES, :] = blank
            diff_acc[top + 2 * rows : top + LANES, :] = blank
        block = pl.ds(yd * 4 * LANES, 4 * LANES)
        base[block, :] = base_acc[block, :].astype(BF16)
        diff[block, :] = diff_acc[block, :].astype(BF16)
        copies.append(pltpu.make_async_copy(base.at[block, :], base_hbm.at[block, :], sems.at[2 * yd]))
        copies.append(pltpu.make_async_copy(diff.at[block, :], diff_hbm.at[block, :], sems.at[2 * yd + 1]))
        copies[-2].start()
        copies[-1].start()
    for copy in copies:
        copy.wait()


def matmul_kernel(tokens, base_hbm, diff_hbm, out, left, base_w, diff_w, base_acc, diff_acc, both, sems):
    rows, wide = tokens.shape[1:]
    toks = rows // 4
    copies = []
    for j in range(4):
        block = pl.ds(j * wide, wide)
        for source, target in ((base_hbm, base_w), (diff_hbm, diff_w)):
            copies.append(pltpu.make_async_copy(source.at[block, :], target.at[block, :], sems.at[len(copies)]))
            copies[-1].start()
    factor = 1.0 / math.sqrt(HB * 16)
    for xd in range(4):
        s = [tokens[xd * 4 + yd].astype(F32) for yd in range(4)]
        a, b, c, d = s[0] + s[1], s[0] - s[1], s[2] + s[3], s[2] - s[3]
        for j, mixed in enumerate((a + c, b + d, a - c, b - d)):
            left[xd * rows : (xd + 1) * rows, j * wide : (j + 1) * wide] = (mixed * factor).astype(BF16)
    for j in range(4):
        block = slice(j * wide, (j + 1) * wide)
        for k, (weight, total) in enumerate(((base_w, base_acc), (diff_w, diff_acc))):
            copies[2 * j + k].wait()
            part = jnp.dot(left[:, block], weight[block, :], preferred_element_type=F32)
            total[...] = part if j == 0 else total[...] + part
    for xd in range(4):
        for yd in range(4):
            start = xd * rows + yd * toks
            both[0:toks, :] = base_acc[start : start + toks, :]
            both[toks : 2 * toks, :] = diff_acc[start : start + toks, :]
            out[xd * 4 + yd] = both[...].astype(BF16)


def unpad_kernel(parts, out, work):
    toks = parts.shape[1]
    for k in range(4):
        work[k * toks : (k + 1) * toks, :] = parts[k].astype(F32)
    out[...] = work[...].astype(BF16)


def spread_kernel(own, g1, g2, g3, signs, out, block, sems):
    mixed = signs[0] * own[...].astype(F32)
    for k, got in enumerate((g1, g2, g3)):
        mixed = mixed + signs[k + 1] * got[...].astype(F32)
    block[...] = mixed.astype(BF16)
    copies = [pltpu.make_async_copy(block, out.at[k], sems.at[k]) for k in range(out.shape[0])]
    for copy in copies:
        copy.start()
    for copy in copies:
        copy.wait()


def near_kernel(parts, out):
    rows = parts.shape[1]
    for ys in range(4):
        acc = parts[ys].astype(F32)
        for zs in range(1, 4):
            acc = acc + parts[zs * 4 + ys].astype(F32)
        for zd in range(4):
            out[zd, ys * rows : (ys + 1) * rows, :] = acc[:, zd * LANES : (zd + 1) * LANES].astype(BF16)


def far_kernel(parts, place, line, keep, send, both, turn, halves):
    rows = parts.shape[1] // 4
    toks = rows // 2
    score = jnp.zeros((toks, LANES), F32)
    for ys in range(4):
        block = slice(ys * rows, (ys + 1) * rows)
        acc = parts[0, block, :].astype(F32)
        for zs in range(1, 4):
            acc = acc + parts[zs, block, :].astype(F32)
        both[...] = acc
        gap = both[toks : 2 * toks, :]
        score = score + gap * gap
        halves[ys // 2, :, (ys % 2) * LANES : (ys % 2 + 1) * LANES] = both[0:toks, :]
    turn[...] = jnp.zeros_like(turn)
    turn[0:toks, :] = jnp.broadcast_to(jnp.sum(score, axis=1, keepdims=True), (toks, LANES))
    row = turn[...].T[0:1, :]
    for k in range(line.shape[0]):
        line[k] = row
    keep[...] = halves[place[2]].astype(BF16)
    send[...] = halves[1 - place[2]].astype(BF16)


def base_kernel(keep, got, place, base, held):
    toks = keep.shape[0]
    first = place[2] == 0
    mine, theirs = keep[...].astype(F32), got[...].astype(F32)
    held[0:toks, :] = jnp.where(first, mine, theirs)
    held[toks : 2 * toks, :] = jnp.where(first, theirs, mine)
    base[...] = held[...].astype(BF16)


def last_kernel(lines, score):
    toks = score.shape[1] // 2
    rows = []
    for cs in range(2):
        row = lines[cs]
        for k in range(1, lines.shape[0] // 2):
            row = row + lines[2 * k + cs]
        rows.append(row)
    lane = lax.broadcasted_iota(jnp.int32, rows[0].shape, 1)
    both = jnp.where(lane < toks, rows[0], pltpu.roll(rows[1], toks, 1))
    score[...] = both[:, 0 : 2 * toks] * (1.0 / SCORE_DIVISOR)


def trade(value, axis, bit, size=4):
    return lax.ppermute(value, axis, [(i, i ^ bit) for i in range(size)])


def local(activations, weight_codes, scale_index, scale_table, bit_widths):
  place = jnp.stack([lax.axis_index(a) for a in ("x", "zh", "c", "y")]).astype(jnp.int32)
  toks, feat = activations.shape
  store, width = weight_codes.shape
  part = width // 16
  padded = store + 4
  wire = call(
      pack_kernel, jax.ShapeDtypeStruct((16, padded, part), BF16),
      [pl.BlockSpec(memory_space=pl.ANY), VMEM, VMEM],
      [pltpu.VMEM((store, width), jnp.int32), pltpu.VMEM((128, 128), F32), pltpu.VMEM((128, 128), F32),
       pltpu.VMEM((padded, part), F32), pltpu.SemaphoreType.DMA((4,))],
      0, store * width * 6, 60,
  )(weight_codes, scale_index, bit_widths.reshape(store, 1, -1))
  home = lax.all_to_all(wire, ("x", "y"), 0, 0, tiled=True)
  other = trade(home, "c", 1, 2)

  value = call(
      block_kernel, jax.ShapeDtypeStruct((4, toks, 4 * LANES), BF16), [VMEM] * 2,
      [pltpu.VMEM((feat // HB, toks + 4, HB), F32)], 2 * toks * 4096 * HB, 1 << 18, 61,
  )(activations, jnp.asarray(SIGNS, BF16))
  value = lax.all_to_all(value, "zh", 0, 0, tiled=True)
  value = call(
      unpad_kernel, jax.ShapeDtypeStruct((4 * toks, 4 * LANES), BF16), [VMEM],
      [pltpu.VMEM((4 * toks, 4 * LANES), F32)], 0, 1 << 18, 4,
  )(value)
  got = []
  for k in (1, 2, 3):
      got.append(trade(value, "zl", k))
  zl = lax.axis_index("zl")
  common = [zl & (zl ^ k) for k in range(4)]
  signs = jnp.stack([1 - 2 * ((v ^ (v >> 1)) & 1) for v in common]).astype(F32)
  value = pl.pallas_call(
      spread_kernel, out_shape=jax.ShapeDtypeStruct((16,) + value.shape, BF16), in_specs=[VMEM] * 4 + [SMEM],
      out_specs=HBM, scratch_shapes=[pltpu.VMEM(value.shape, BF16), pltpu.SemaphoreType.DMA((16,))],
      name="spread", compiler_params=pltpu.CompilerParams(vmem_limit_bytes=8 << 20),
      cost_estimate=pl.CostEstimate(flops=0, bytes_accessed=1 << 21, transcendentals=0),
  )(value, *got, signs)
  tokens = lax.all_to_all(value, ("x", "y"), 0, 0, tiled=True)

  base_w, diff_w = pl.pallas_call(
      lambda *refs: weight_kernel(store, *refs),
      out_shape=[jax.ShapeDtypeStruct((16 * LANES, part), BF16)] * 2,
      in_specs=[VMEM, VMEM, SMEM, SMEM], out_specs=[HBM, HBM],
      scratch_shapes=[pltpu.VMEM((128, 128), F32)] + [pltpu.VMEM((16 * LANES, part), F32)] * 2
      + [pltpu.VMEM((16 * LANES, part), BF16)] * 2 + [pltpu.SemaphoreType.DMA((8,))],
      name="weights", compiler_params=pltpu.CompilerParams(vmem_limit_bytes=52 << 20),
      cost_estimate=pl.CostEstimate(flops=feat * part * 20, bytes_accessed=feat * part * 6, transcendentals=0),
  )(home, other, scale_table, place)
  sums = call(
      matmul_kernel, jax.ShapeDtypeStruct((16, 2 * toks, part), BF16),
      [VMEM, HBM, HBM],
      [pltpu.VMEM((16 * toks, 16 * LANES), BF16)] + [pltpu.VMEM((16 * LANES, part), BF16)] * 2
      + [pltpu.VMEM((16 * toks, part), F32)] * 2 + [pltpu.VMEM((2 * toks, part), F32), pltpu.SemaphoreType.DMA((8,))],
      4 * 16 * toks * feat * part, feat * part * 4 + 16 * toks * feat * 2, 52,
  )(tokens, base_w, diff_w)
  near = lax.all_to_all(sums, ("zl", "y"), 0, 0, tiled=True)
  wave = call(
      near_kernel, jax.ShapeDtypeStruct((4, 8 * toks, LANES), BF16), [VMEM], (),
      32 * toks * part, 64 * toks * part, 8,
  )(near)
  far = lax.all_to_all(wave, "zh", 0, 0, tiled=True)
  line, keep, send = call(
      far_kernel,
      [jax.ShapeDtypeStruct((32, 1, LANES), F32)] + [jax.ShapeDtypeStruct((toks, 2 * LANES), BF16)] * 2,
      [VMEM, SMEM],
      [pltpu.VMEM((2 * toks, LANES), F32), pltpu.VMEM((LANES, LANES), F32), pltpu.VMEM((2, toks, 2 * LANES), F32)],
      32 * toks * part, 40 * toks * part, 4,
  )(far, place)
  lines = lax.all_to_all(line, ("x", "zh", "c"), 0, 0, tiled=True)
  got = trade(send, "c", 1, 2)
  base = call(
      base_kernel, jax.ShapeDtypeStruct((2 * toks, 2 * LANES), BF16), [VMEM, VMEM, SMEM],
      [pltpu.VMEM((2 * toks, 2 * LANES), F32)], 1 << 12, 1 << 16, 4,
  )(keep, got, place)
  scores = call(last_kernel, jax.ShapeDtypeStruct((1, 2 * toks), F32), [VMEM], (), 1 << 12, 1 << 14, 4)(lines)
  return base, scores


def solution(mesh):
    fine = Mesh(mesh.devices.reshape(SIZES), AXES)
    dp, tensor = ("x", "zh", "c"), ("zl", "y")
    return jax.shard_map(
        local, mesh=fine,
        in_specs=(P(dp, tensor), P(tensor + dp, None), P(tensor + dp, None), P(), P(None, tensor + dp, None)),
        out_specs=(P(tensor, dp), P(None, tensor)),
        check_vma=False,
    )
```
